512 devices in a mesh: lat: 4 (over x_hi, core), lon: 32 (over z, x_lo), tensor: 4 (over y).
Axes of the slice: x: 4 (x_hi: 2, x_lo: 2; x = x_hi * 2 + x_lo), y: 4, z: 16, core: 2. Of those that a mesh axis runs over, the one named last changes fastest.
Arguments:
- fields: bfloat16 [64, 768, 256], P('lat', 'lon'), may hold values from -8 to 8
- norm_gain1: float32 [256], replicated, may hold values from 0.5 to 1.5
- w_qkv: bfloat16 [256, 3, 8, 32], P(None, None, 'tensor'), may hold values from -0.1875 to 0.1875
- logit_scale: float32 [8], P('tensor'), may hold values from 1 to 64
- w_out: bfloat16 [8, 32, 256], P('tensor'), may hold values from -0.375 to 0.375
- attn_keep: int32 [64, 256], P('lat'), may hold values 0 or 1
- dw_kernel: bfloat16 [7, 7, 256], replicated, may hold values from -0.875 to 0.875
- norm_gain2: float32 [256], replicated, may hold values from 0.5 to 1.5
- w_up: bfloat16 [256, 1024], P(None, 'tensor'), may hold values from -0.375 to 0.375
- w_down: bfloat16 [1024, 256], P('tensor'), may hold values from -0.1875 to 0.1875
- mlp_keep: int32 [64, 256], P('lat'), may hold values 0 or 1
Outputs:
- result: bfloat16 [64, 768, 256], P('lat', 'lon')
The draws below stay inside these ranges and needn't reach their ends.
All inputs are finite; a program needn't handle non-finite values. No bound on the sum of `attn_keep` or of `mlp_keep` on one device may be relied on, other than what follows from the above.
Results may differ from the reference program's by a relative error of at most 0.014.
Values may be sent and summed in bfloat16 or wider, within the bound.
A program may use at most 64 MiB of HBM per device.

```python
import math
import jax
import jax.numpy as jnp
from jax import lax

CHANNELS = 256
HEADS = 8
FFN_WIDTH = 1024
KERNEL = 7
HEAD_SIZE = 32
LAT = 64
LON = 768


def draw_fields(key, part):
    base_key = jax.random.fold_in(key, 0)
    base = jax.random.normal(base_key, (LAT, LON, CHANNELS), jnp.float32)
    return jnp.clip(base, -8.0, 8.0).astype(jnp.bfloat16)


def draw_w_qkv(key, part):
    bound = 3.0 / math.sqrt(CHANNELS)
    raw = jax.random.normal(key, (CHANNELS, 3, HEADS, HEAD_SIZE), jnp.float32) * (1.0 / math.sqrt(CHANNELS))
    return jnp.clip(raw, -bound, bound).astype(jnp.bfloat16)


def draw_logit_scale(key, part):
    values = jnp.exp(jax.random.uniform(key, (HEADS,), jnp.float32, math.log(1.5), math.log(4.0)))
    return jnp.clip(values, 1.0, 64.0)


def touch_ends(result, stream_key, low, largest):
    extent = result.shape
    index_at = [jax.random.randint(jax.random.fold_in(stream_key, axis), (), 0, extent[axis]) for axis in range(len(extent))]
    result = result.at[tuple(index_at)].set(low)
    longest = extent.index(max(extent))
    index_at[longest] = (index_at[longest] + 1) % extent[longest]
    return result.at[tuple(index_at)].set(largest)


def block_scale(own_key, dims, shards, low, high):
    factor_of, own = 1.0, jax.random.fold_in(own_key, 6)
    for position, shards_of in shards:
        steps = jnp.exp(jax.random.uniform(jax.random.fold_in(own, position), (shards_of,), jnp.float32, low / len(shards), high / len(shards)))
        factor_of = factor_of * jnp.repeat(steps, dims[position] // shards_of).reshape([-1 if axis == position else 1 for axis in range(len(dims))])
    return factor_of


def bell_draw(key, extent, scale, most, shards=(), kind=jnp.bfloat16):
    level = block_scale(key, extent, shards, -0.22, 0.18) if shards else 1.0
    array = jax.random.normal(key, extent, jnp.float32) * scale * level
    return jnp.minimum(jnp.maximum(array, -most), most).astype(kind)


def setup_inputs(seed: int = 0) -> dict:
    splits = jax.random.split(jax.random.key(seed), 12)
    fields = draw_fields(jax.random.fold_in(splits[11], 71), 0)
    norm_gain1 = jnp.clip(jax.random.uniform(splits[1], (CHANNELS,), jnp.float32, 0.5, 1.5), 0.5, 1.5)
    w_qkv = draw_w_qkv(jax.random.fold_in(splits[11], 71), 0)
    logit_scale = draw_logit_scale(jax.random.fold_in(splits[11], 71), 0)
    w_out = bell_draw(splits[4], (HEADS, HEAD_SIZE, CHANNELS), CHANNELS ** -0.5, 0.375, ((0, 4),))
    attn_keep = touch_ends((jax.random.randint(splits[5], (LAT, CHANNELS), 0, 10) < 9).astype(jnp.int32), jax.random.fold_in(splits[5], 1), 0, 1)
    dw_kernel = bell_draw(splits[6], (KERNEL, KERNEL, CHANNELS), (KERNEL * KERNEL) ** -0.5, 0.875)
    norm_gain2 = jnp.clip(jax.random.uniform(splits[7], (CHANNELS,), jnp.float32, 0.5, 1.5), 0.5, 1.5)
    w_up = bell_draw(splits[8], (CHANNELS, FFN_WIDTH), CHANNELS ** -0.5, 0.375, ((1, 4),))
    w_down = bell_draw(splits[9], (FFN_WIDTH, CHANNELS), FFN_WIDTH ** -0.5, 0.1875, ((0, 4),))
    mlp_keep = touch_ends((jax.random.randint(splits[10], (LAT, CHANNELS), 0, 10) < 9).astype(jnp.int32), jax.random.fold_in(splits[10], 1), 0, 1)
    return {"fields": fields, "norm_gain1": norm_gain1, "w_qkv": w_qkv, "logit_scale": logit_scale, "w_out": w_out, "attn_keep": attn_keep, "dw_kernel": dw_kernel, "norm_gain2": norm_gain2, "w_up": w_up, "w_down": w_down, "mlp_keep": mlp_keep}


ln_eps = 1e-05
keep_prob = 0.9

def layer_norm(values, gain):
    widened = values.astype(jnp.float32)
    center = lax.optimization_barrier(jnp.mean(widened, axis=-1, keepdims=True))
    spread = lax.optimization_barrier(jnp.mean(jnp.square(widened - center), axis=-1, keepdims=True))
    return (widened - center) * lax.rsqrt(spread + ln_eps) * gain

def depthwise(wide, kernel, rows, cols):
    kernel_f = kernel.astype(jnp.float32)
    wide_f = wide.astype(jnp.float32)
    width = kernel.shape[0]
    total = jnp.zeros((rows, cols, wide.shape[2]), jnp.float32)
    for row_off in range(width):
        for col_off in range(width):
            total = total + kernel_f[row_off, col_off] * wide_f[row_off:row_off + rows, col_off:col_off + cols]
    return total

def reference(fields, norm_gain1, w_qkv, logit_scale, w_out, attn_keep, dw_kernel, norm_gain2, w_up, w_down, mlp_keep):
    logit_coef = logit_scale * (1.0 / math.sqrt(HEAD_SIZE))
    qkv_matrix = w_qkv.reshape(CHANNELS, 3 * HEADS * HEAD_SIZE)
    out_matrix = w_out.reshape(HEADS * HEAD_SIZE, CHANNELS)

    def attend_head(item):
        queries, keys, values, coef_one = item
        scores = jnp.dot(queries, keys.T, preferred_element_type=jnp.float32) * coef_one
        top = lax.optimization_barrier(jnp.max(scores, axis=-1, keepdims=True))
        weights = jnp.exp(scores - top)
        total = lax.optimization_barrier(jnp.sum(weights, axis=-1, keepdims=True))
        return (jnp.dot(weights.astype(jnp.bfloat16), values, preferred_element_type=jnp.float32) / total).astype(jnp.bfloat16)

    def attend_row(item):
        field_row, keep_row = item
        normed = layer_norm(field_row, norm_gain1).astype(jnp.bfloat16)
        projected = jnp.dot(normed, qkv_matrix, preferred_element_type=jnp.float32).astype(jnp.bfloat16)
        projected = projected.reshape(LON, 3, HEADS, HEAD_SIZE)
        by_head = jnp.transpose(projected, (1, 2, 0, 3))
        mixed = lax.map(attend_head, (by_head[0], by_head[1], by_head[2], logit_coef))
        joined = jnp.transpose(mixed, (1, 0, 2)).reshape(LON, HEADS * HEAD_SIZE)
        attended = jnp.dot(joined, out_matrix, preferred_element_type=jnp.float32)
        return (field_row.astype(jnp.float32) + attended * (keep_row.astype(jnp.float32) / keep_prob)).astype(jnp.bfloat16)
    stream = lax.map(attend_row, (fields, attn_keep))
    margin = KERNEL // 2
    padded = jnp.pad(stream, ((margin, margin), (0, 0), (0, 0)))
    padded = jnp.concatenate([padded[:, LON - margin:], padded, padded[:, :margin]], axis=1)

    def finish_row(item):
        row_index, stream_row, keep_row = item
        slab = lax.dynamic_slice_in_dim(padded, row_index, KERNEL, 0)
        spatial = depthwise(slab, dw_kernel, 1, LON).astype(jnp.bfloat16)[0]
        normed2 = layer_norm(spatial, norm_gain2).astype(jnp.bfloat16)
        hidden = jax.nn.gelu(jnp.dot(normed2, w_up, preferred_element_type=jnp.float32), approximate=False).astype(jnp.bfloat16)
        ffn = jnp.dot(hidden, w_down, preferred_element_type=jnp.float32)
        return (stream_row.astype(jnp.float32) + ffn * (keep_row.astype(jnp.float32) / keep_prob)).astype(jnp.bfloat16)
    return lax.map(finish_row, (jnp.arange(LAT, dtype=jnp.int32), stream, mlp_keep))
```

```python
import functools
import math

import jax
import jax.numpy as jnp
from jax import lax
from jax.experimental import pallas as pl
from jax.experimental.pallas import tpu as pltpu
from jax.sharding import PartitionSpec as P

ln_eps = 1e-05
keep_prob = 0.9
LANES = 128
SUB = 8
MESH = pl.DeviceIdType.MESH
f32 = jnp.float32
bf16 = jnp.bfloat16


def layer_norm(values, gain):
    center = jnp.mean(values, axis=-1, keepdims=True)
    shifted = values - center
    spread = jnp.mean(jnp.square(shifted), axis=-1, keepdims=True)
    return (shifted * lax.rsqrt(spread + ln_eps) * gain).astype(bf16)


def kernel(
    n_lat,
    n_lon,
    n_ten,
    fields,
    gain1,
    w_qkv,
    logit_scale,
    w_out,
    attn_keep,
    dw_kernel,
    gain2,
    w_up,
    w_down,
    mlp_keep,
    out,
    proj_w,
    sent,
    got,
    values,
    mixed,
    joined,
    out_w,
    out_wide,
    up_w,
    down_w,
    taps,
    ext,
    ext_f,
    done,
    go_sem,
    send_a,
    recv_a,
    send_b,
    send_b_own,
    recv_b,
    send_w,
    recv_w,
    own_w,
    send_h,
    recv_h,
    send_o,
    recv_o,
):
    rows, cols, channels = fields.shape
    heads = w_qkv.shape[1]
    head_size = w_qkv.shape[2]
    groups = cols // SUB
    quarter = rows // n_ten
    all_heads = heads * n_ten
    size = dw_kernel.shape[0]
    margin = size // 2
    halves = channels // LANES
    bands = n_lat * n_ten

    lat = lax.axis_index("lat")
    lon = lax.axis_index("lon")
    ten = lax.axis_index("tensor")
    band = lat * n_ten + ten

    def band_at(step):
        there = lax.rem(band + step + bands, bands)
        return {"lat": there // n_ten, "tensor": lax.rem(there, n_ten)}

    def lon_at(step):
        return lax.rem(lon + step + n_lon, n_lon)

    def ten_at(step):
        return lax.rem(ten + step, n_ten)

    def far_first(i):
        return n_lon // 2 + ((i + 1) // 2) * (1 - 2 * lax.rem(i, 2))

    barrier = pltpu.get_barrier_semaphore()

    def greet(i, carry):
        pl.semaphore_signal(
            barrier, inc=1, device_id={"lon": lon_at(far_first(i))}, device_id_type=MESH
        )
        return carry

    lax.fori_loop(0, n_lon - 1, greet, 0)
    for step in range(1, n_ten):
        pl.semaphore_signal(
            barrier, inc=1, device_id={"tensor": ten_at(step)}, device_id_type=MESH
        )
    for step in (-1, 1):
        pl.semaphore_signal(barrier, inc=1, device_id=band_at(step), device_id_type=MESH)

    proj_w[...] = jnp.zeros_like(proj_w)
    for head in range(heads):
        for which in range(3):
            proj_w[pl.ds(head * LANES + which * head_size, head_size), :] = w_qkv[which, head]
    normed = layer_norm(fields[...].reshape(rows * cols, channels).astype(f32), gain1[...])
    projected = lax.dot_general(
        normed, proj_w[...], (((1,), (1,)), ((), ())), preferred_element_type=f32
    ).astype(bf16)
    projected = projected.reshape(rows, groups, SUB, heads * LANES)
    for row in range(rows):
        for head in range(heads):
            sent[row * heads + head] = projected[row, :, :, head * LANES : (head + 1) * LANES]

    pl.semaphore_wait(barrier, n_lon - 1 + n_ten - 1 + 2)

    def send_pair(i, carry):
        peer = lon_at(far_first(i))
        pltpu.make_async_remote_copy(
            src_ref=sent.at[peer],
            dst_ref=got.at[:, lon],
            send_sem=send_a,
            recv_sem=recv_a,
            device_id={"lon": peer},
            device_id_type=MESH,
        ).start()
        return carry

    lax.fori_loop(0, n_lon - 1, send_pair, 0)
    pltpu.make_async_copy(sent.at[lon], got.at[:, lon], recv_a).start()

    for step in range(1, n_ten):
        pl.semaphore_signal(
            go_sem, inc=1, device_id={"tensor": ten_at(step)}, device_id_type=MESH
        )
    for step in (-1, 1):
        pl.semaphore_signal(go_sem, inc=1, device_id=band_at(step), device_id_type=MESH)

    pairs_w = ((w_out, out_w), (w_up, up_w), (w_down, down_w))
    weight_copies = []
    for kind, (mine, whole) in enumerate(pairs_w):
        for step in range(1, n_ten):
            copy = pltpu.make_async_remote_copy(
                src_ref=mine,
                dst_ref=whole.at[ten],
                send_sem=send_w.at[kind, step - 1],
                recv_sem=recv_w.at[kind, step - 1],
                device_id={"tensor": ten_at(step)},
                device_id_type=MESH,
            )
            copy.start()
            weight_copies.append(copy)
        pltpu.make_async_copy(mine, whole.at[ten], own_w.at[kind]).start()

    for row_off in range(size):
        line = dw_kernel[row_off].astype(f32)
        for col_off in range(size):
            for half in range(halves):
                taps[half, row_off * size + col_off] = jnp.broadcast_to(
                    line[col_off : col_off + 1, half * LANES : (half + 1) * LANES],
                    (SUB, LANES),
                )

    pltpu.make_async_copy(got, got, recv_a).wait()
    keys = groups * n_lon * SUB
    gathered = got[...].reshape(keys, LANES)
    wide = gathered.astype(f32)
    lane = lax.broadcasted_iota(jnp.int32, (keys, LANES), 1)
    at_keys = (lane >= head_size) & (lane < 2 * head_size)
    queries = jnp.where(at_keys, pltpu.roll(wide, head_size, 1), 0.0).astype(bf16)
    for group in range(groups):
        low, high = group * head_size, (group + 1) * head_size
        shift = (low - 2 * head_size) % LANES
        moved = pltpu.roll(wide, shift, 1) if shift else wide
        inside = (lane >= low) & (lane < high)
        last = LANES if group == groups - 1 else high
        values[group, :, :LANES] = jnp.where(inside, moved, 0.0).astype(bf16)
        values[group, :, LANES:] = jnp.where((lane >= low) & (lane < last), 1.0, 0.0).astype(bf16)
    pair_head = lax.rem(lon, heads)
    pair_row = lon // heads
    scale = logit_scale[0]
    for head in range(1, heads):
        scale = jnp.where(pair_head == head, logit_scale[head], scale)
    coef = scale * (math.log2(math.e) / math.sqrt(head_size))
    span = n_lon * SUB
    total = jnp.zeros((span, 2 * LANES), f32)
    for group in range(groups):
        scores = lax.dot_general(
            queries[group * span : (group + 1) * span],
            gathered,
            (((1,), (1,)), ((), ())),
            preferred_element_type=f32,
        )
        top = jnp.max(scores, axis=-1, keepdims=True)
        weights = jnp.exp2((scores - top) * coef).astype(bf16)
        total = total + jnp.dot(weights, values[group], preferred_element_type=f32)
    mixed[...] = (
        (total[:, :LANES] / total[:, LANES:]).astype(bf16).reshape(n_lon, SUB, LANES)
    )

    owner = pair_row // quarter
    slot_row = lax.rem(pair_row, quarter)
    slot_head = ten * heads + pair_head
    pl.semaphore_wait(go_sem, n_ten - 1 + 2)

    def send_back(i, carry):
        peer = lon_at(far_first(i))
        pltpu.make_async_remote_copy(
            src_ref=mixed.at[peer],
            dst_ref=joined.at[slot_row, slot_head],
            send_sem=send_b,
            recv_sem=recv_b,
            device_id={"lon": peer, "tensor": owner},
            device_id_type=MESH,
        ).start()
        return carry

    lax.fori_loop(0, n_lon - 1, send_back, 0)

    @pl.when(owner == ten)
    def _():
        pltpu.make_async_copy(mixed.at[lon], joined.at[slot_row, slot_head], recv_b).start()

    own_back = pltpu.make_async_remote_copy(
        src_ref=mixed.at[lon],
        dst_ref=joined.at[slot_row, slot_head],
        send_sem=send_b_own,
        recv_sem=recv_b,
        device_id={"tensor": owner},
        device_id_type=MESH,
    )

    @pl.when(owner != ten)
    def _():
        own_back.start()

    out_wide[...] = jnp.zeros_like(out_wide)
    pltpu.make_async_copy(w_out, out_w.at[ten], own_w.at[0]).wait()
    for step in range(1, n_ten):
        weight_copies[step - 1].wait_recv()
    for head in range(all_heads):
        block = out_w[head // heads, head % heads]
        for group in range(groups):
            out_wide[
                pl.ds(head * LANES + group * head_size, head_size),
                pl.ds(group * channels, channels),
            ] = block

    pltpu.make_async_copy(joined, joined, recv_b).wait()
    packed = jnp.concatenate(
        [joined[:, head].reshape(quarter * SUB, LANES) for head in range(all_heads)], axis=-1
    )
    attended = jnp.dot(packed, out_wide[...], preferred_element_type=f32)
    for row in range(quarter):
        at = ten * quarter + row
        factor = attn_keep[pl.ds(at, 1), :].astype(f32) / keep_prob
        block = fields[at].astype(f32)
        for group in range(groups):
            piece = attended[
                row * SUB : (row + 1) * SUB, group * channels : (group + 1) * channels
            ]
            ext[margin + row, pl.ds((group + 1) * SUB, SUB), :] = (
                block[group * SUB : (group + 1) * SUB] + piece * factor
            ).astype(bf16)

    first, final = pl.ds(SUB, SUB), pl.ds(cols, SUB)
    left, right, middle = pl.ds(0, SUB), pl.ds(cols + SUB, SUB), pl.ds(SUB, cols)
    top_rows, low_rows = pl.ds(margin, margin), pl.ds(quarter, margin)
    above, below, own_rows = (
        pl.ds(0, margin),
        pl.ds(margin + quarter, margin),
        pl.ds(margin, quarter),
    )
    halo_copies = []
    for band_step, src_rows, dst_rows in (
        (-1, top_rows, below),
        (1, low_rows, above),
        (0, own_rows, own_rows),
    ):
        for lon_step, src_cols, dst_cols in (
            (-1, first, right),
            (1, final, left),
            (0, middle, middle),
        ):
            if band_step == 0 and lon_step == 0:
                continue
            where = dict(band_at(band_step)) if band_step else {}
            if lon_step:
                where["lon"] = lon_at(lon_step)
            index = len(halo_copies)
            copy = pltpu.make_async_remote_copy(
                src_ref=ext.at[src_rows, src_cols],
                dst_ref=ext.at[dst_rows, dst_cols],
                send_sem=send_h.at[index],
                recv_sem=recv_h.at[index],
                device_id=where,
                device_id_type=MESH,
            )
            copy.start()
            halo_copies.append(copy)
    for copy in halo_copies:
        copy.wait_recv()

    for row in range(quarter + 2 * margin):
        line = ext[row].astype(f32)
        if row < margin:
            line = jnp.where(band > 0, line, 0.0)
        if row >= margin + quarter:
            line = jnp.where(band < bands - 1, line, 0.0)
        for half in range(halves):
            ext_f[half, row] = line[:, half * LANES : (half + 1) * LANES]
    parts = []
    for half in range(halves):
        sums = [jnp.zeros((cols, LANES), f32) for _ in range(quarter)]
        for col_off in range(size):
            tap = [
                jnp.concatenate([taps[half, row_off * size + col_off]] * groups, axis=0)
                for row_off in range(size)
            ]
            for row in range(quarter + 2 * margin):
                line = ext_f[half, row, pl.ds(SUB - margin + col_off, cols), :]
                for i in range(quarter):
                    if 0 <= row - i < size:
                        sums[i] = sums[i] + tap[row - i] * line
        parts.append(jnp.concatenate(sums, axis=0))
    spatial = jnp.concatenate(parts, axis=-1).astype(bf16).astype(f32)

    normed2 = layer_norm(spatial, gain2[...])
    for kind in (1, 2):
        mine, whole = pairs_w[kind]
        pltpu.make_async_copy(mine, whole.at[ten], own_w.at[kind]).wait()
        for step in range(1, n_ten):
            weight_copies[kind * (n_ten - 1) + step - 1].wait_recv()
    ffn = jnp.zeros((quarter * cols, channels), f32)
    for part in range(n_ten):
        inner = jnp.dot(normed2, up_w[part], preferred_element_type=f32)
        hidden = (0.5 * inner * (1.0 + lax.erf(inner * math.sqrt(0.5)))).astype(bf16)
        ffn = ffn + jnp.dot(hidden, down_w[part], preferred_element_type=f32)
    for row in range(quarter):
        factor = mlp_keep[pl.ds(ten * quarter + row, 1), :].astype(f32) / keep_prob
        stream = ext[margin + row, middle, :].astype(f32)
        done[row] = (stream + ffn[row * cols : (row + 1) * cols] * factor).astype(bf16)

    mine = pl.ds(ten * quarter, quarter)
    out_copies = []
    for step in range(1, n_ten):
        copy = pltpu.make_async_remote_copy(
            src_ref=done,
            dst_ref=out.at[mine],
            send_sem=send_o.at[step - 1],
            recv_sem=recv_o.at[step - 1],
            device_id={"tensor": ten_at(step)},
            device_id_type=MESH,
        )
        copy.start()
        out_copies.append(copy)
    own_out = pltpu.make_async_copy(done, out.at[mine], send_o.at[n_ten - 1])
    own_out.start()

    pltpu.make_async_copy(sent.at[: n_lon - 1], sent.at[: n_lon - 1], send_a).wait()
    pltpu.make_async_copy(mixed.at[: n_lon - 1], mixed.at[: n_lon - 1], send_b).wait()

    @pl.when(owner != ten)
    def _():
        own_back.wait_send()

    for copy in weight_copies + halo_copies + out_copies:
        copy.wait_send()
    own_out.wait()
    for copy in out_copies:
        copy.wait_recv()


def shards(sizes, fields, gain1, w_qkv, logit_scale, w_out, attn_keep, dw_kernel, gain2, w_up, w_down, mlp_keep):
    n_lat, n_lon, n_ten = sizes
    rows, cols, channels = fields.shape
    heads, head_size = w_qkv.shape[2:]
    hidden = w_up.shape[1]
    groups, quarter, size = cols // SUB, rows // n_ten, dw_kernel.shape[0]
    margin, halves = size // 2, channels // LANES
    span = quarter + 2 * margin
    vmem = pl.BlockSpec(memory_space=pltpu.VMEM)
    hbm = pl.BlockSpec(memory_space=pl.ANY)
    smem = pl.BlockSpec(memory_space=pltpu.SMEM)
    dma = pltpu.SemaphoreType.DMA
    return pl.pallas_call(
        functools.partial(kernel, n_lat, n_lon, n_ten),
        out_shape=jax.ShapeDtypeStruct(fields.shape, bf16),
        in_specs=[vmem, vmem, vmem, smem, hbm, vmem, vmem, vmem, hbm, hbm, vmem],
        out_specs=hbm,
        scratch_shapes=[
            pltpu.VMEM((heads * LANES, channels), bf16),
            pltpu.VMEM((n_lon, groups, SUB, LANES), bf16),
            pltpu.VMEM((groups, n_lon, SUB, LANES), bf16),
            pltpu.VMEM((groups, groups * n_lon * SUB, 2 * LANES), bf16),
            pltpu.VMEM((n_lon, SUB, LANES), bf16),
            pltpu.VMEM((quarter, heads * n_ten, SUB, LANES), bf16),
            pltpu.VMEM((n_ten,) + w_out.shape, bf16),
            pltpu.VMEM((heads * n_ten * LANES, groups * channels), bf16),
            pltpu.VMEM((n_ten, channels, hidden), bf16),
            pltpu.VMEM((n_ten, hidden, channels), bf16),
            pltpu.VMEM((halves, size * size, SUB, LANES), f32),
            pltpu.VMEM((span, cols + 2 * SUB, channels), bf16),
            pltpu.VMEM((halves, span, cols + 2 * SUB, LANES), f32),
            pltpu.VMEM((quarter, cols, channels), bf16),
            pltpu.SemaphoreType.REGULAR,
            dma, dma, dma, dma, dma,
            dma((3, n_ten - 1)),
            dma((3, n_ten - 1)),
            dma((3,)),
            dma((8,)),
            dma((8,)),
            dma((n_ten,)),
            dma((n_ten - 1,)),
        ],
        compiler_params=pltpu.CompilerParams(
            collective_id=0, has_side_effects=True, vmem_limit_bytes=48 << 20
        ),
    )(
        fields,
        gain1.reshape(1, channels),
        w_qkv.transpose(1, 2, 3, 0),
        logit_scale,
        w_out,
        attn_keep,
        dw_kernel,
        gain2.reshape(1, channels),
        w_up,
        w_down,
        mlp_keep,
    )


def solution(mesh):
    sizes = tuple(mesh.shape[axis] for axis in ("lat", "lon", "tensor"))
    placed = (
        P("lat", "lon", None),
        P(),
        P(None, None, "tensor", None),
        P("tensor"),
        P("tensor", None, None),
        P("lat", None),
        P(),
        P(),
        P(None, "tensor"),
        P("tensor", None),
        P("lat", None),
    )
    return jax.shard_map(
        functools.partial(shards, sizes),
        mesh=mesh,
        in_specs=placed,
        out_specs=P("lat", "lon", None),
        check_vma=False,
    )
```

```python
import functools
import math

import jax
import jax.numpy as jnp
from jax import lax
from jax.experimental import pallas as pl
from jax.experimental.pallas import tpu as pltpu
from jax.sharding import PartitionSpec as P

ln_eps = 1e-05
keep_prob = 0.9
LANES = 128
SUB = 8
MESH = pl.DeviceIdType.MESH
f32 = jnp.float32
bf16 = jnp.bfloat16


def layer_norm(values, gain):
    center = jnp.mean(values, axis=-1, keepdims=True)
    shifted = values - center
    spread = jnp.mean(jnp.square(shifted), axis=-1, keepdims=True)
    return (shifted * lax.rsqrt(spread + ln_eps) * gain).astype(bf16)


def kernel(
    n_lat,
    n_lon,
    n_ten,
    fields_hbm,
    gain1_hbm,
    w_qkv_hbm,
    logit_scale_hbm,
    w_out,
    attn_keep_hbm,
    dw_kernel_hbm,
    gain2_hbm,
    w_up,
    w_down,
    mlp_keep_hbm,
    out,
    fields,
    gain1,
    w_qkv,
    logit_scale,
    attn_keep,
    dw_kernel,
    gain2,
    mlp_keep,
    proj_w,
    sent,
    got,
    values,
    mixed,
    joined,
    out_w,
    out_wide,
    up_w,
    down_w,
    taps,
    ext,
    ext_f,
    side,
    done,
    fetch_sem,
    go_sem,
    send_a,
    recv_a,
    send_b,
    send_b_own,
    recv_b,
    send_w,
    recv_w,
    send_p,
    recv_p,
    send_s,
    recv_s,
    own_w,
    send_h,
    recv_h,
    send_o,
    recv_o,
):
    rows, cols, channels = fields.shape
    heads = w_qkv.shape[1]
    head_size = w_qkv.shape[2]
    groups = cols // SUB
    quarter = rows // n_ten
    all_heads = heads * n_ten
    size = dw_kernel.shape[0]
    margin = size // 2
    halves = channels // LANES
    bands = n_lat * n_ten

    lat = lax.axis_index("lat")
    lon = lax.axis_index("lon")
    ten = lax.axis_index("tensor")
    core = lax.rem(lat, 2)
    sibling = {"lat": lat + 1 - 2 * core}

    def turned(which_lat, place):
        odd = lax.rem(which_lat, 2)
        return place + odd * (n_ten - 1 - 2 * place)

    part = turned(lat, ten)
    band = lat * n_ten + part

    def band_at(step):
        there = lax.rem(band + step + bands, bands)
        there_lat = there // n_ten
        return {"lat": there_lat, "tensor": turned(there_lat, lax.rem(there, n_ten))}

    def lon_at(step):
        return lax.rem(lon + step + n_lon, n_lon)

    def ten_at(step):
        return lax.rem(ten + step, n_ten)

    def far_first(i):
        return n_lon // 2 + ((i + 1) // 2) * (1 - 2 * lax.rem(i, 2))

    fetches = [
        pltpu.make_async_copy(source, target, fetch_sem.at[index])
        for index, (source, target) in enumerate(
            (
                (fields_hbm, fields),
                (w_qkv_hbm, w_qkv),
                (gain1_hbm, gain1),
                (dw_kernel_hbm, dw_kernel),
                (logit_scale_hbm, logit_scale),
                (attn_keep_hbm, attn_keep),
                (gain2_hbm, gain2),
                (mlp_keep_hbm, mlp_keep),
            )
        )
    ]
    for fetch in fetches[:3]:
        fetch.start()

    barrier = pltpu.get_barrier_semaphore()

    def greet(i, carry):
        pl.semaphore_signal(
            barrier, inc=1, device_id={"lon": lon_at(far_first(i))}, device_id_type=MESH
        )
        return carry

    lax.fori_loop(0, n_lon - 1, greet, 0)
    for step in range(1, n_ten):
        pl.semaphore_signal(
            barrier, inc=1, device_id={"tensor": ten_at(step)}, device_id_type=MESH
        )
    for step in (-1, 1):
        pl.semaphore_signal(barrier, inc=1, device_id=band_at(step), device_id_type=MESH)
    pl.semaphore_signal(barrier, inc=1, device_id=sibling, device_id_type=MESH)

    for fetch in fetches[3:]:
        fetch.start()

    proj_w[...] = jnp.zeros_like(proj_w)
    for fetch in fetches[:3]:
        fetch.wait()
    for head in range(heads):
        for which in range(3):
            proj_w[pl.ds(head * LANES + which * head_size, head_size), :] = w_qkv[which, head]
    normed = layer_norm(fields[...].reshape(rows * cols, channels).astype(f32), gain1[...])
    projected = lax.dot_general(
        normed, proj_w[...], (((1,), (1,)), ((), ())), preferred_element_type=f32
    ).astype(bf16)
    projected = projected.reshape(rows, groups, SUB, heads * LANES)
    for row in range(rows):
        for head in range(heads):
            place = row % quarter * n_ten + row // quarter
            sent[place * heads + head] = projected[row, :, :, head * LANES : (head + 1) * LANES]

    pl.semaphore_wait(barrier, n_lon - 1 + n_ten - 1 + 3)

    def send_pair(i, carry):
        peer = lon_at(far_first(i))
        pltpu.make_async_remote_copy(
            src_ref=sent.at[peer],
            dst_ref=got.at[:, lon],
            send_sem=send_a,
            recv_sem=recv_a,
            device_id={"lon": peer},
            device_id_type=MESH,
        ).start()
        return carry

    lax.fori_loop(0, n_lon - 1, send_pair, 0)
    pltpu.make_async_copy(sent.at[lon], got.at[:, lon], recv_a).start()

    for step in range(1, n_ten):
        pl.semaphore_signal(
            go_sem, inc=1, device_id={"tensor": ten_at(step)}, device_id_type=MESH
        )
    for step in (-1, 1):
        pl.semaphore_signal(go_sem, inc=1, device_id=band_at(step), device_id_type=MESH)

    def half_of(ref):
        half = ref.shape[0] // 2
        return ref.at[pl.ds(core * half, half)]

    pairs_w = ((w_out, out_w), (w_up, up_w), (w_down, down_w))
    weight_copies, weight_passes, weight_own = [], [], []
    for kind, (mine, whole) in enumerate(pairs_w):
        for step in range(1, n_ten):
            copy = pltpu.make_async_remote_copy(
                src_ref=half_of(mine),
                dst_ref=half_of(whole.at[ten]),
                send_sem=send_w.at[kind, step - 1],
                recv_sem=recv_w.at[kind, step - 1],
                device_id={"tensor": ten_at(step)},
                device_id_type=MESH,
            )
            copy.start()
            weight_copies.append(copy)
            arrived = half_of(whole.at[ten_at(n_ten - step)])
            weight_passes.append(
                pltpu.make_async_remote_copy(
                    src_ref=arrived,
                    dst_ref=arrived,
                    send_sem=send_p.at[kind, step - 1],
                    recv_sem=recv_p.at[kind, step - 1],
                    device_id=sibling,
                    device_id_type=MESH,
                )
            )
        own = pltpu.make_async_copy(mine, whole.at[ten], own_w.at[kind])
        own.start()
        weight_own.append(own)

    def weights_here(kind):
        weight_own[kind].wait()
        for step in range(1, n_ten):
            weight_passes[kind * (n_ten - 1) + step - 1].wait_recv()

    own_part = pl.ds(part * quarter, quarter)
    side_copies = []
    for index, (step, start) in enumerate(((1, cols - SUB), (-1, 0))):
        copy = pltpu.make_async_remote_copy(
            src_ref=fields.at[own_part, pl.ds(start, SUB)],
            dst_ref=side.at[index],
            send_sem=send_s.at[index],
            recv_sem=recv_s.at[index],
            device_id={"lon": lon_at(step)},
            device_id_type=MESH,
        )
        copy.start()
        side_copies.append(copy)

    for fetch in fetches[3:]:
        fetch.wait()
    for row_off in range(size):
        line = dw_kernel[row_off].astype(f32)
        for col_off in range(size):
            for half in range(halves):
                taps[half, row_off * size + col_off] = jnp.broadcast_to(
                    line[col_off : col_off + 1, half * LANES : (half + 1) * LANES],
                    (SUB, LANES),
                )

    pltpu.make_async_copy(got, got, recv_a).wait()
    for copy, onward in zip(weight_copies, weight_passes):
        copy.wait_recv()
        onward.start()
    keys = groups * n_lon * SUB
    gathered = got[...].reshape(keys, LANES)
    wide = gathered.astype(f32)
    lane = lax.broadcasted_iota(jnp.int32, (keys, LANES), 1)
    at_keys = (lane >= head_size) & (lane < 2 * head_size)
    queries = jnp.where(at_keys, pltpu.roll(wide, head_size, 1), 0.0)
    by_group = queries.reshape(groups, n_lon, SUB, LANES)
    left_side = jnp.concatenate([by_group[-1, -1:], by_group[-1, :-1]], axis=0)
    right_side = jnp.concatenate([by_group[0, 1:], by_group[0, :1]], axis=0)
    place = lax.broadcasted_iota(jnp.int32, left_side.shape, 1)
    beside = jnp.where(place >= SUB // 2, left_side, right_side)
    span = n_lon * SUB
    queries = [by_group[group].reshape(span, LANES).astype(bf16) for group in range(groups)]
    queries.append(beside.reshape(span, LANES).astype(bf16))
    for group in range(groups + 1):
        low, high = group * head_size, (group + 1) * head_size
        shift = (low - 2 * head_size) % LANES
        moved = pltpu.roll(wide, shift, 1) if shift else wide
        inside = (lane >= low) & (lane < high)
        values[group, :, :LANES] = jnp.where(inside, moved, 0.0).astype(bf16)
        values[group, :, LANES:] = jnp.where(inside, 1.0, 0.0).astype(bf16)
    pair_head = lax.rem(lon, heads)
    pair_place = lon // heads
    scale = logit_scale[0]
    for head in range(1, heads):
        scale = jnp.where(pair_head == head, logit_scale[head], scale)
    coef = scale * (math.log2(math.e) / math.sqrt(head_size))
    total = jnp.zeros((span, 2 * LANES), f32)
    for group in range(groups + 1):
        scores = lax.dot_general(
            queries[group],
            gathered,
            (((1,), (1,)), ((), ())),
            preferred_element_type=f32,
        )
        top = jnp.max(scores, axis=-1, keepdims=True)
        weights = jnp.exp2((scores - top) * coef).astype(bf16)
        total = total + jnp.dot(weights, values[group], preferred_element_type=f32)
    mixed[...] = (
        (total[:, :LANES] / total[:, LANES:]).astype(bf16).reshape(n_lon, SUB, LANES)
    )

    owner = turned(lat, lax.rem(pair_place, n_ten))
    slot_row = pair_place // n_ten
    slot_head = ten * heads + pair_head
    pl.semaphore_wait(go_sem, n_ten - 1 + 2)

    def send_back(i, carry):
        peer = lon_at(far_first(i))
        pltpu.make_async_remote_copy(
            src_ref=mixed.at[peer],
            dst_ref=joined.at[slot_row, slot_head],
            send_sem=send_b,
            recv_sem=recv_b,
            device_id={"lon": peer, "tensor": owner},
            device_id_type=MESH,
        ).start()
        return carry

    lax.fori_loop(0, n_lon - 1, send_back, 0)

    @pl.when(owner == ten)
    def _():
        pltpu.make_async_copy(mixed.at[lon], joined.at[slot_row, slot_head], recv_b).start()

    own_back = pltpu.make_async_remote_copy(
        src_ref=mixed.at[lon],
        dst_ref=joined.at[slot_row, slot_head],
        send_sem=send_b_own,
        recv_sem=recv_b,
        device_id={"tensor": owner},
        device_id_type=MESH,
    )

    @pl.when(owner != ten)
    def _():
        own_back.start()

    out_wide[...] = jnp.zeros_like(out_wide)
    weights_here(0)
    for head in range(all_heads):
        block = out_w[head // heads, head % heads]
        for group in range(groups + 1):
            out_wide[
                pl.ds(head * LANES + group * head_size, head_size),
                pl.ds(group * channels, channels),
            ] = block

    pltpu.make_async_copy(joined, joined, recv_b).wait()
    packed = jnp.concatenate(
        [joined[:, head].reshape(quarter * SUB, LANES) for head in range(all_heads)], axis=-1
    )
    attended = jnp.dot(packed, out_wide[...], preferred_element_type=f32)
    for copy in side_copies:
        copy.wait_recv()
    place = lax.broadcasted_iota(jnp.int32, (SUB, channels), 0)
    for row in range(quarter):
        at = part * quarter + row
        factor = attn_keep[pl.ds(at, 1), :].astype(f32) / keep_prob
        block = fields[at].astype(f32)
        for group in range(groups + 1):
            piece = attended[
                row * SUB : (row + 1) * SUB, group * channels : (group + 1) * channels
            ]
            if group < groups:
                base = block[group * SUB : (group + 1) * SUB]
            else:
                base = jnp.where(
                    place >= SUB // 2, side[0, row].astype(f32), side[1, row].astype(f32)
                )
            stream = (base + piece * factor).astype(bf16)
            if group < groups:
                ext[margin + row, pl.ds((group + 1) * SUB, SUB), :] = stream
            else:
                ext[margin + row, pl.ds(0, SUB), :] = stream
                ext[margin + row, pl.ds(cols + SUB, SUB), :] = stream

    middle = pl.ds(SUB, cols)
    halo_copies = []
    for index, (step, source, target) in enumerate(
        ((-1, margin, margin + quarter), (1, quarter, 0))
    ):
        copy = pltpu.make_async_remote_copy(
            src_ref=ext.at[pl.ds(source, margin)],
            dst_ref=ext.at[pl.ds(target, margin)],
            send_sem=send_h.at[index],
            recv_sem=recv_h.at[index],
            device_id=band_at(step),
            device_id_type=MESH,
        )
        copy.start()
        halo_copies.append(copy)
    for copy in halo_copies:
        copy.wait_recv()

    for row in range(quarter + 2 * margin):
        line = ext[row].astype(f32)
        if row < margin:
            line = jnp.where(band > 0, line, 0.0)
        if row >= margin + quarter:
            line = jnp.where(band < bands - 1, line, 0.0)
        for half in range(halves):
            ext_f[half, row] = line[:, half * LANES : (half + 1) * LANES]
    parts = []
    for half in range(halves):
        sums = [jnp.zeros((cols, LANES), f32) for _ in range(quarter)]
        for col_off in range(size):
            tap = [
                jnp.concatenate([taps[half, row_off * size + col_off]] * groups, axis=0)
                for row_off in range(size)
            ]
            for row in range(quarter + 2 * margin):
                line = ext_f[half, row, pl.ds(SUB - margin + col_off, cols), :]
                for i in range(quarter):
                    if 0 <= row - i < size:
                        sums[i] = sums[i] + tap[row - i] * line
        parts.append(jnp.concatenate(sums, axis=0))
    spatial = jnp.concatenate(parts, axis=-1).astype(bf16).astype(f32)

    normed2 = layer_norm(spatial, gain2[...])
    weights_here(1)
    weights_here(2)
    ffn = jnp.zeros((quarter * cols, channels), f32)
    for index in range(n_ten):
        inner = jnp.dot(normed2, up_w[index], preferred_element_type=f32)
        hidden = (0.5 * inner * (1.0 + lax.erf(inner * math.sqrt(0.5)))).astype(bf16)
        ffn = ffn + jnp.dot(hidden, down_w[index], preferred_element_type=f32)
    for row in range(quarter):
        factor = mlp_keep[pl.ds(part * quarter + row, 1), :].astype(f32) / keep_prob
        stream = ext[margin + row, middle, :].astype(f32)
        done[row] = (stream + ffn[row * cols : (row + 1) * cols] * factor).astype(bf16)

    out_copies = []
    for step in range(1, n_ten):
        copy = pltpu.make_async_remote_copy(
            src_ref=done,
            dst_ref=out.at[own_part],
            send_sem=send_o.at[step - 1],
            recv_sem=recv_o.at[step - 1],
            device_id={"tensor": ten_at(step)},
            device_id_type=MESH,
        )
        copy.start()
        out_copies.append(copy)
    own_out = pltpu.make_async_copy(done, out.at[own_part], send_o.at[n_ten - 1])
    own_out.start()

    pltpu.make_async_copy(sent.at[: n_lon - 1], sent.at[: n_lon - 1], send_a).wait()
    pltpu.make_async_copy(mixed.at[: n_lon - 1], mixed.at[: n_lon - 1], send_b).wait()

    @pl.when(owner != ten)
    def _():
        own_back.wait_send()

    for copy in weight_copies + weight_passes + side_copies + halo_copies + out_copies:
        copy.wait_send()
    own_out.wait()
    for copy in out_copies:
        copy.wait_recv()


def shards(sizes, fields, gain1, w_qkv, logit_scale, w_out, attn_keep, dw_kernel, gain2, w_up, w_down, mlp_keep):
    n_lat, n_lon, n_ten = sizes
    rows, cols, channels = fields.shape
    heads, head_size = w_qkv.shape[2:]
    hidden = w_up.shape[1]
    groups, quarter, size = cols // SUB, rows // n_ten, dw_kernel.shape[0]
    margin, halves = size // 2, channels // LANES
    span = quarter + 2 * margin
    hbm = pl.BlockSpec(memory_space=pltpu.HBM)
    dma = pltpu.SemaphoreType.DMA
    return pl.pallas_call(
        functools.partial(kernel, n_lat, n_lon, n_ten),
        out_shape=jax.ShapeDtypeStruct(fields.shape, bf16),
        in_specs=[hbm] * 11,
        out_specs=pl.BlockSpec(memory_space=pl.ANY),
        scratch_shapes=[
            pltpu.VMEM(fields.shape, bf16),
            pltpu.VMEM((1, channels), f32),
            pltpu.VMEM((3, heads, head_size, channels), bf16),
            pltpu.SMEM(logit_scale.shape, f32),
            pltpu.VMEM(attn_keep.shape, jnp.int32),
            pltpu.VMEM(dw_kernel.shape, bf16),
            pltpu.VMEM((1, channels), f32),
            pltpu.VMEM(mlp_keep.shape, jnp.int32),
            pltpu.VMEM((heads * LANES, channels), bf16),
            pltpu.VMEM((n_lon, groups, SUB, LANES), bf16),
            pltpu.VMEM((groups, n_lon, SUB, LANES), bf16),
            pltpu.VMEM((groups + 1, groups * n_lon * SUB, 2 * LANES), bf16),
            pltpu.VMEM((n_lon, SUB, LANES), bf16),
            pltpu.VMEM((quarter, heads * n_ten, SUB, LANES), bf16),
            pltpu.VMEM((n_ten,) + w_out.shape, bf16),
            pltpu.VMEM((heads * n_ten * LANES, (groups + 1) * channels), bf16),
            pltpu.VMEM((n_ten, channels, hidden), bf16),
            pltpu.VMEM((n_ten, hidden, channels), bf16),
            pltpu.VMEM((halves, size * size, SUB, LANES), f32),
            pltpu.VMEM((span, cols + 2 * SUB, channels), bf16),
            pltpu.VMEM((halves, span, cols + 2 * SUB, LANES), f32),
            pltpu.VMEM((2, quarter, SUB, channels), bf16),
            pltpu.VMEM((quarter, cols, channels), bf16),
            dma((8,)),
            pltpu.SemaphoreType.REGULAR,
            dma, dma, dma, dma, dma,
            dma((3, n_ten - 1)),
            dma((3, n_ten - 1)),
            dma((3, n_ten - 1)),
            dma((3, n_ten - 1)),
            dma((2,)),
            dma((2,)),
            dma((3,)),
            dma((2,)),
            dma((2,)),
            dma((n_ten,)),
            dma((n_ten - 1,)),
        ],
        compiler_params=pltpu.CompilerParams(
            collective_id=0, has_side_effects=True, vmem_limit_bytes=56 << 20
        ),
    )(
        *(
            pltpu.with_memory_space_constraint(operand, pltpu.HBM)
            for operand in (
                fields,
                gain1.reshape(1, channels),
                w_qkv.transpose(1, 2, 3, 0),
                logit_scale,
                w_out,
                attn_keep,
                dw_kernel,
                gain2.reshape(1, channels),
                w_up,
                w_down,
                mlp_keep,
            )
        )
    )


def solution(mesh):
    sizes = tuple(mesh.shape[axis] for axis in ("lat", "lon", "tensor"))
    placed = (
        P("lat", "lon", None),
        P(),
        P(None, None, "tensor", None),
        P("tensor"),
        P("tensor", None, None),
        P("lat", None),
        P(),
        P(),
        P(None, "tensor"),
        P("tensor", None),
        P("lat", None),
    )
    return jax.shard_map(
        functools.partial(shards, sizes),
        mesh=mesh,
        in_specs=placed,
        out_specs=P("lat", "lon", None),
        check_vma=False,
    )
```

```python
import functools
import math

import jax
import jax.numpy as jnp
from jax import lax
from jax.experimental import pallas as pl
from jax.experimental.pallas import tpu as pltpu
from jax.sharding import PartitionSpec as P

ln_eps = 1e-05
keep_prob = 0.9
LANES = 128
SUB = 8
MESH = pl.DeviceIdType.MESH
f32 = jnp.float32
bf16 = jnp.bfloat16


def layer_norm(values, gain):
    center = jnp.mean(values, axis=-1, keepdims=True)
    shifted = values - center
    spread = jnp.mean(jnp.square(shifted), axis=-1, keepdims=True)
    return (shifted * lax.rsqrt(spread + ln_eps) * gain).astype(bf16)


def kernel(
    n_lat,
    n_lon,
    n_ten,
    fields_hbm,
    gain1_hbm,
    w_qkv_hbm,
    logit_scale_hbm,
    w_out,
    attn_keep_hbm,
    dw_kernel_hbm,
    gain2_hbm,
    w_up,
    w_down,
    mlp_keep_hbm,
    out,
    fields,
    gain1,
    w_qkv,
    logit_scale,
    attn_keep,
    dw_kernel,
    gain2,
    mlp_keep,
    proj_w,
    sent,
    got,
    values,
    mixed,
    joined,
    out_w,
    out_wide,
    up_w,
    down_w,
    taps,
    ext,
    ext_f,
    side,
    done,
    fetch_sem,
    go_sem,
    send_a,
    recv_a,
    send_b,
    send_b_own,
    recv_b,
    send_w,
    recv_w,
    send_p,
    recv_p,
    send_s,
    recv_s,
    own_w,
    send_h,
    recv_h,
    send_o,
    recv_o,
):
    rows, cols, channels = fields.shape
    heads = w_qkv.shape[1]
    head_size = w_qkv.shape[2]
    groups = cols // SUB
    quarter = rows // n_ten
    all_heads = heads * n_ten
    size = dw_kernel.shape[0]
    margin = size // 2
    halves = channels // LANES
    bands = n_lat * n_ten
    spot_of = (14, 1, 15, 0, 8, 7, 9, 6, 10, 5, 11, 4, 12, 3, 13, 2)
    row_of = (3, 1, 15, 13, 11, 9, 7, 5, 4, 6, 8, 10, 12, 14, 0, 2)

    lat = lax.axis_index("lat")
    lon = lax.axis_index("lon")
    ten = lax.axis_index("tensor")
    core = lax.rem(lat, 2)
    sibling = {"lat": lat + 1 - 2 * core}

    def turned(which_lat, place):
        odd = lax.rem(which_lat, 2)
        return place + odd * (n_ten - 1 - 2 * place)

    part = turned(lat, ten)
    band = lat * n_ten + part

    def band_at(step):
        there = lax.rem(band + step + bands, bands)
        there_lat = there // n_ten
        return {"lat": there_lat, "tensor": turned(there_lat, lax.rem(there, n_ten))}

    def lon_at(step):
        return lax.rem(lon + step + n_lon, n_lon)

    def ten_at(step):
        return lax.rem(ten + step, n_ten)

    def far_first(i):
        return n_lon // 2 + ((i + 1) // 2) * (1 - 2 * lax.rem(i, 2))

    def by_core(i):
        return far_first(i + core * (n_lon - 2 - 2 * i))

    fetches = [
        pltpu.make_async_copy(source, target, fetch_sem.at[index])
        for index, (source, target) in enumerate(
            (
                (fields_hbm, fields),
                (w_qkv_hbm, w_qkv),
                (gain1_hbm, gain1),
                (dw_kernel_hbm, dw_kernel),
                (logit_scale_hbm, logit_scale),
                (attn_keep_hbm, attn_keep),
                (gain2_hbm, gain2),
                (mlp_keep_hbm, mlp_keep),
            )
        )
    ]
    for fetch in fetches[:3]:
        fetch.start()

    barrier = pltpu.get_barrier_semaphore()

    def greet(i, carry):
        pl.semaphore_signal(
            barrier, inc=1, device_id={"lon": lon_at(far_first(i))}, device_id_type=MESH
        )
        return carry

    lax.fori_loop(0, n_lon - 1, greet, 0)
    for step in range(1, n_ten):
        pl.semaphore_signal(
            barrier, inc=1, device_id={"tensor": ten_at(step)}, device_id_type=MESH
        )
    for step in (-1, 1):
        pl.semaphore_signal(barrier, inc=1, device_id=band_at(step), device_id_type=MESH)
    pl.semaphore_signal(barrier, inc=1, device_id=sibling, device_id_type=MESH)

    for fetch in fetches[3:]:
        fetch.start()

    proj_w[...] = jnp.zeros_like(proj_w)
    for fetch in fetches[:3]:
        fetch.wait()
    for head in range(heads):
        for which in range(3):
            proj_w[pl.ds(head * LANES + which * head_size, head_size), :] = w_qkv[which, head]
    normed = layer_norm(fields[...].reshape(rows * cols, channels).astype(f32), gain1[...])
    projected = lax.dot_general(
        normed, proj_w[...], (((1,), (1,)), ((), ())), preferred_element_type=f32
    ).astype(bf16)
    projected = projected.reshape(rows, groups, SUB, heads * LANES)
    for row in range(rows):
        for head in range(heads):
            place = spot_of[row]
            sent[place * heads + head] = projected[row, :, :, head * LANES : (head + 1) * LANES]

    pl.semaphore_wait(barrier, n_lon - 1 + n_ten - 1 + 3)

    def send_pair(i, carry):
        peer = lon_at(by_core(i))
        pltpu.make_async_remote_copy(
            src_ref=sent.at[peer],
            dst_ref=got.at[:, lon],
            send_sem=send_a,
            recv_sem=recv_a,
            device_id={"lon": peer},
            device_id_type=MESH,
        ).start()
        return carry

    lax.fori_loop(0, n_lon - 1, send_pair, 0)
    pltpu.make_async_copy(sent.at[lon], got.at[:, lon], recv_a).start()

    for step in range(1, n_ten):
        pl.semaphore_signal(
            go_sem, inc=1, device_id={"tensor": ten_at(step)}, device_id_type=MESH
        )
    for step in (-1, 1):
        pl.semaphore_signal(go_sem, inc=1, device_id=band_at(step), device_id_type=MESH)

    def half_of(ref):
        half = ref.shape[0] // 2
        return ref.at[pl.ds(core * half, half)]

    pairs_w = ((w_out, out_w), (w_up, up_w), (w_down, down_w))
    weight_copies, weight_passes, weight_own = [], [], []
    for kind, (mine, whole) in enumerate(pairs_w):
        for step in range(1, n_ten):
            copy = pltpu.make_async_remote_copy(
                src_ref=half_of(mine),
                dst_ref=half_of(whole.at[ten]),
                send_sem=send_w.at[kind, step - 1],
                recv_sem=recv_w.at[kind, step - 1],
                device_id={"tensor": ten_at(step)},
                device_id_type=MESH,
            )
            copy.start()
            weight_copies.append(copy)
            arrived = half_of(whole.at[ten_at(n_ten - step)])
            weight_passes.append(
                pltpu.make_async_remote_copy(
                    src_ref=arrived,
                    dst_ref=arrived,
                    send_sem=send_p.at[kind, step - 1],
                    recv_sem=recv_p.at[kind, step - 1],
                    device_id=sibling,
                    device_id_type=MESH,
                )
            )
        own = pltpu.make_async_copy(mine, whole.at[ten], own_w.at[kind])
        own.start()
        weight_own.append(own)

    def weights_here(kind):
        weight_own[kind].wait()
        for step in range(1, n_ten):
            weight_passes[kind * (n_ten - 1) + step - 1].wait_recv()

    own_part = pl.ds(part * quarter, quarter)
    side_copies = []
    for index, (step, start) in enumerate(((1, cols - SUB), (-1, 0))):
        copy = pltpu.make_async_remote_copy(
            src_ref=fields.at[own_part, pl.ds(start, SUB)],
            dst_ref=side.at[index],
            send_sem=send_s.at[index],
            recv_sem=recv_s.at[index],
            device_id={"lon": lon_at(step)},
            device_id_type=MESH,
        )
        copy.start()
        side_copies.append(copy)

    for fetch in fetches[3:]:
        fetch.wait()
    for row_off in range(size):
        line = dw_kernel[row_off].astype(f32)
        for col_off in range(size):
            for half in range(halves):
                taps[half, row_off * size + col_off] = jnp.broadcast_to(
                    line[col_off : col_off + 1, half * LANES : (half + 1) * LANES],
                    (SUB, LANES),
                )

    pltpu.make_async_copy(got, got, recv_a).wait()
    for copy, onward in zip(weight_copies, weight_passes):
        copy.wait_recv()
        onward.start()
    keys = groups * n_lon * SUB
    gathered = got[...].reshape(keys, LANES)
    wide = gathered.astype(f32)
    lane = lax.broadcasted_iota(jnp.int32, (keys, LANES), 1)
    at_keys = (lane >= head_size) & (lane < 2 * head_size)
    queries = jnp.where(at_keys, pltpu.roll(wide, head_size, 1), 0.0)
    by_group = queries.reshape(groups, n_lon, SUB, LANES)
    left_side = jnp.concatenate([by_group[-1, -1:], by_group[-1, :-1]], axis=0)
    right_side = jnp.concatenate([by_group[0, 1:], by_group[0, :1]], axis=0)
    place = lax.broadcasted_iota(jnp.int32, left_side.shape, 1)
    beside = jnp.where(place >= SUB // 2, left_side, right_side)
    span = n_lon * SUB
    queries = [by_group[group].reshape(span, LANES).astype(bf16) for group in range(groups)]
    queries.append(beside.reshape(span, LANES).astype(bf16))
    for group in range(groups + 1):
        low, high = group * head_size, (group + 1) * head_size
        shift = (low - 2 * head_size) % LANES
        moved = pltpu.roll(wide, shift, 1) if shift else wide
        inside = (lane >= low) & (lane < high)
        values[group, :, :LANES] = jnp.where(inside, moved, 0.0).astype(bf16)
        values[group, :, LANES:] = jnp.where(inside, 1.0, 0.0).astype(bf16)
    pair_head = lax.rem(lon, heads)
    pair_place = lon // heads
    scale = logit_scale[0]
    for head in range(1, heads):
        scale = jnp.where(pair_head == head, logit_scale[head], scale)
    coef = scale * (math.log2(math.e) / math.sqrt(head_size))
    total = jnp.zeros((span, 2 * LANES), f32)
    for group in range(groups + 1):
        scores = lax.dot_general(
            queries[group],
            gathered,
            (((1,), (1,)), ((), ())),
            preferred_element_type=f32,
        )
        top = jnp.max(scores, axis=-1, keepdims=True)
        weights = jnp.exp2((scores - top) * coef).astype(bf16)
        total = total + jnp.dot(weights, values[group], preferred_element_type=f32)
    mixed[...] = (
        (total[:, :LANES] / total[:, LANES:]).astype(bf16).reshape(n_lon, SUB, LANES)
    )

    pair_row = row_of[0]
    for index in range(1, rows):
        pair_row = jnp.where(pair_place == index, row_of[index], pair_row)
    owner = turned(lat, pair_row // quarter)
    slot_row = lax.rem(pair_row, quarter)
    slot_head = ten * heads + pair_head
    pl.semaphore_wait(go_sem, n_ten - 1 + 2)

    def send_back(i, carry):
        peer = lon_at(far_first(i))
        pltpu.make_async_remote_copy(
            src_ref=mixed.at[peer],
            dst_ref=joined.at[slot_row, slot_head],
            send_sem=send_b,
            recv_sem=recv_b,
            device_id={"lon": peer, "tensor": owner},
            device_id_type=MESH,
        ).start()
        return carry

    lax.fori_loop(0, n_lon - 1, send_back, 0)

    @pl.when(owner == ten)
    def _():
        pltpu.make_async_copy(mixed.at[lon], joined.at[slot_row, slot_head], recv_b).start()

    own_back = pltpu.make_async_remote_copy(
        src_ref=mixed.at[lon],
        dst_ref=joined.at[slot_row, slot_head],
        send_sem=send_b_own,
        recv_sem=recv_b,
        device_id={"tensor": owner},
        device_id_type=MESH,
    )

    @pl.when(owner != ten)
    def _():
        own_back.start()

    out_wide[...] = jnp.zeros_like(out_wide)
    weights_here(0)
    for head in range(all_heads):
        block = out_w[head // heads, head % heads]
        for group in range(groups + 1):
            out_wide[
                pl.ds(head * LANES + group * head_size, head_size),
                pl.ds(group * channels, channels),
            ] = block

    pltpu.make_async_copy(joined, joined, recv_b).wait()
    packed = jnp.concatenate(
        [joined[:, head].reshape(quarter * SUB, LANES) for head in range(all_heads)], axis=-1
    )
    attended = jnp.dot(packed, out_wide[...], preferred_element_type=f32)
    for copy in side_copies:
        copy.wait_recv()
    place = lax.broadcasted_iota(jnp.int32, (SUB, channels), 0)
    for row in range(quarter):
        at = part * quarter + row
        factor = attn_keep[pl.ds(at, 1), :].astype(f32) / keep_prob
        block = fields[at].astype(f32)
        for group in range(groups + 1):
            piece = attended[
                row * SUB : (row + 1) * SUB, group * channels : (group + 1) * channels
            ]
            if group < groups:
                base = block[group * SUB : (group + 1) * SUB]
            else:
                base = jnp.where(
                    place >= SUB // 2, side[0, row].astype(f32), side[1, row].astype(f32)
                )
            stream = (base + piece * factor).astype(bf16)
            if group < groups:
                ext[margin + row, pl.ds((group + 1) * SUB, SUB), :] = stream
            else:
                ext[margin + row, pl.ds(0, SUB), :] = stream

    middle = pl.ds(SUB, cols)
    halo_copies = []
    for index, (step, source, target) in enumerate(
        ((-1, margin, margin + quarter), (1, quarter, 0))
    ):
        copy = pltpu.make_async_remote_copy(
            src_ref=ext.at[pl.ds(source, margin)],
            dst_ref=ext.at[pl.ds(target, margin)],
            send_sem=send_h.at[index],
            recv_sem=recv_h.at[index],
            device_id=band_at(step),
            device_id_type=MESH,
        )
        halo_copies.append(copy)
    has_above, has_below = band > 0, band < bands - 1

    @pl.when(has_above)
    def _():
        halo_copies[0].start()

    @pl.when(has_below)
    def _():
        halo_copies[1].start()

    @pl.when(jnp.logical_not(has_above))
    def _():
        ext[pl.ds(0, margin)] = jnp.zeros((margin,) + ext.shape[1:], bf16)

    @pl.when(jnp.logical_not(has_below))
    def _():
        ext[pl.ds(margin + quarter, margin)] = jnp.zeros((margin,) + ext.shape[1:], bf16)

    @pl.when(has_above)
    def _():
        halo_copies[1].wait_recv()

    @pl.when(has_below)
    def _():
        halo_copies[0].wait_recv()

    for row in range(quarter + 2 * margin):
        line = ext[row].astype(f32)
        for half in range(halves):
            piece = line[:, half * LANES : (half + 1) * LANES]
            ext_f[half, row, pl.ds(0, cols + SUB), :] = piece
            ext_f[half, row, pl.ds(cols + SUB, SUB), :] = piece[:SUB]
    parts = []
    for half in range(halves):
        sums = [jnp.zeros((cols, LANES), f32) for _ in range(quarter)]
        for col_off in range(size):
            tap = [
                jnp.concatenate([taps[half, row_off * size + col_off]] * groups, axis=0)
                for row_off in range(size)
            ]
            for row in range(quarter + 2 * margin):
                line = ext_f[half, row, pl.ds(SUB - margin + col_off, cols), :]
                for i in range(quarter):
                    if 0 <= row - i < size:
                        sums[i] = sums[i] + tap[row - i] * line
        parts.append(jnp.concatenate(sums, axis=0))
    spatial = jnp.concatenate(parts, axis=-1).astype(bf16).astype(f32)

    normed2 = layer_norm(spatial, gain2[...])
    weights_here(1)
    weights_here(2)
    ffn = jnp.zeros((quarter * cols, channels), f32)
    for index in range(n_ten):
        inner = jnp.dot(normed2, up_w[index], preferred_element_type=f32)
        hidden = (0.5 * inner * (1.0 + lax.erf(inner * math.sqrt(0.5)))).astype(bf16)
        ffn = ffn + jnp.dot(hidden, down_w[index], preferred_element_type=f32)
    for row in range(quarter):
        factor = mlp_keep[pl.ds(part * quarter + row, 1), :].astype(f32) / keep_prob
        stream = ext[margin + row, middle, :].astype(f32)
        done[row] = (stream + ffn[row * cols : (row + 1) * cols] * factor).astype(bf16)

    out_copies = []
    for index in range(n_ten - 1):
        target = index + (index >= ten).astype(jnp.int32)
        slot = lax.rem(target - ten + n_ten - 1, n_ten)
        copy = pltpu.make_async_remote_copy(
            src_ref=done,
            dst_ref=out.at[own_part],
            send_sem=send_o.at[index],
            recv_sem=recv_o.at[slot],
            device_id={"tensor": target},
            device_id_type=MESH,
        )
        copy.start()
        out_copies.append(copy)
    own_out = pltpu.make_async_copy(done, out.at[own_part], send_o.at[n_ten - 1])
    own_out.start()

    @pl.when(has_above)
    def _():
        halo_copies[0].wait_send()

    @pl.when(has_below)
    def _():
        halo_copies[1].wait_send()

    pltpu.make_async_copy(sent.at[: n_lon - 1], sent.at[: n_lon - 1], send_a).wait()
    pltpu.make_async_copy(mixed.at[: n_lon - 1], mixed.at[: n_lon - 1], send_b).wait()

    @pl.when(owner != ten)
    def _():
        own_back.wait_send()

    for copy in weight_copies + weight_passes + side_copies + out_copies:
        copy.wait_send()
    own_out.wait()
    for slot in range(n_ten - 1):
        pltpu.make_async_copy(done, out.at[own_part], recv_o.at[slot]).wait()


def shards(sizes, fields, gain1, w_qkv, logit_scale, w_out, attn_keep, dw_kernel, gain2, w_up, w_down, mlp_keep):
    n_lat, n_lon, n_ten = sizes
    rows, cols, channels = fields.shape
    heads, head_size = w_qkv.shape[2:]
    hidden = w_up.shape[1]
    groups, quarter, size = cols // SUB, rows // n_ten, dw_kernel.shape[0]
    margin, halves = size // 2, channels // LANES
    span = quarter + 2 * margin
    hbm = pl.BlockSpec(memory_space=pltpu.HBM)
    dma = pltpu.SemaphoreType.DMA
    return pl.pallas_call(
        functools.partial(kernel, n_lat, n_lon, n_ten),
        out_shape=jax.ShapeDtypeStruct(fields.shape, bf16),
        in_specs=[hbm] * 11,
        out_specs=pl.BlockSpec(memory_space=pl.ANY),
        scratch_shapes=[
            pltpu.VMEM(fields.shape, bf16),
            pltpu.VMEM((1, channels), f32),
            pltpu.VMEM((3, heads, head_size, channels), bf16),
            pltpu.SMEM(logit_scale.shape, f32),
            pltpu.VMEM(attn_keep.shape, jnp.int32),
            pltpu.VMEM(dw_kernel.shape, bf16),
            pltpu.VMEM((1, channels), f32),
            pltpu.VMEM(mlp_keep.shape, jnp.int32),
            pltpu.VMEM((heads * LANES, channels), bf16),
            pltpu.VMEM((n_lon, groups, SUB, LANES), bf16),
            pltpu.VMEM((groups, n_lon, SUB, LANES), bf16),
            pltpu.VMEM((groups + 1, groups * n_lon * SUB, 2 * LANES), bf16),
            pltpu.VMEM((n_lon, SUB, LANES), bf16),
            pltpu.VMEM((quarter, heads * n_ten, SUB, LANES), bf16),
            pltpu.VMEM((n_ten,) + w_out.shape, bf16),
            pltpu.VMEM((heads * n_ten * LANES, (groups + 1) * channels), bf16),
            pltpu.VMEM((n_ten, channels, hidden), bf16),
            pltpu.VMEM((n_ten, hidden, channels), bf16),
            pltpu.VMEM((halves, size * size, SUB, LANES), f32),
            pltpu.VMEM((span, cols + SUB, channels), bf16),
            pltpu.VMEM((halves, span, cols + 2 * SUB, LANES), f32),
            pltpu.VMEM((2, quarter, SUB, channels), bf16),
            pltpu.VMEM((quarter, cols, channels), bf16),
            dma((8,)),
            pltpu.SemaphoreType.REGULAR,
            dma, dma, dma, dma, dma,
            dma((3, n_ten - 1)),
            dma((3, n_ten - 1)),
            dma((3, n_ten - 1)),
            dma((3, n_ten - 1)),
            dma((2,)),
            dma((2,)),
            dma((3,)),
            dma((2,)),
            dma((2,)),
            dma((n_ten,)),
            dma((n_ten - 1,)),
        ],
        compiler_params=pltpu.CompilerParams(
            collective_id=0, has_side_effects=True, vmem_limit_bytes=32 << 20
        ),
    )(
        *(
            pltpu.with_memory_space_constraint(operand, pltpu.HBM)
            for operand in (
                fields,
                gain1.reshape(1, channels),
                w_qkv.transpose(1, 2, 3, 0),
                logit_scale,
                w_out,
                attn_keep,
                dw_kernel,
                gain2.reshape(1, channels),
                w_up,
                w_down,
                mlp_keep,
            )
        )
    )


def solution(mesh):
    sizes = tuple(mesh.shape[axis] for axis in ("lat", "lon", "tensor"))
    placed = (
        P("lat", "lon", None),
        P(),
        P(None, None, "tensor", None),
        P("tensor"),
        P("tensor", None, None),
        P("lat", None),
        P(),
        P(),
        P(None, "tensor"),
        P("tensor", None),
        P("lat", None),
    )
    return jax.shard_map(
        functools.partial(shards, sizes),
        mesh=mesh,
        in_specs=placed,
        out_specs=P("lat", "lon", None),
        check_vma=False,
    )
```

```python
import functools
import math

import jax
import jax.numpy as jnp
from jax import lax
from jax.experimental import pallas as pl
from jax.experimental.pallas import tpu as pltpu
from jax.sharding import PartitionSpec as P

ln_eps = 1e-05
keep_prob = 0.9
LANES = 128
SUB = 8
MESH = pl.DeviceIdType.MESH
f32 = jnp.float32
bf16 = jnp.bfloat16


def layer_norm(values, gain):
    center = jnp.mean(values, axis=-1, keepdims=True)
    shifted = values - center
    spread = jnp.mean(jnp.square(shifted), axis=-1, keepdims=True)
    return (shifted * lax.rsqrt(spread + ln_eps) * gain).astype(bf16)


def kernel(
    n_lat,
    n_lon,
    n_ten,
    fields_hbm,
    gain1_hbm,
    w_qkv_hbm,
    logit_scale_hbm,
    w_out,
    attn_keep_hbm,
    dw_kernel_hbm,
    gain2_hbm,
    w_up,
    w_down,
    mlp_keep_hbm,
    out,
    fields,
    gain1,
    w_qkv,
    logit_scale,
    attn_keep,
    dw_kernel,
    gain2,
    mlp_keep,
    proj_w,
    sent,
    got,
    values,
    mixed,
    joined,
    out_w,
    out_wide,
    up_w,
    down_w,
    taps,
    ext,
    ext_f,
    side,
    done,
    fetch_sem,
    go_sem,
    send_a,
    recv_a,
    send_b,
    send_b_own,
    recv_b,
    send_w,
    recv_w,
    send_p,
    recv_p,
    send_s,
    recv_s,
    own_w,
    send_h,
    recv_h,
    send_o,
    recv_o,
):
    rows, cols, channels = fields.shape
    heads = w_qkv.shape[1]
    head_size = w_qkv.shape[2]
    groups = cols // SUB
    quarter = rows // n_ten
    all_heads = heads * n_ten
    size = dw_kernel.shape[0]
    margin = size // 2
    halves = channels // LANES
    bands = n_lat * n_ten
    spot_of = (14, 1, 15, 0, 8, 7, 9, 6, 10, 5, 11, 4, 12, 3, 13, 2)
    row_of = (3, 1, 15, 13, 11, 9, 7, 5, 4, 6, 8, 10, 12, 14, 0, 2)

    lat = lax.axis_index("lat")
    lon = lax.axis_index("lon")
    ten = lax.axis_index("tensor")
    core = lax.rem(lat, 2)
    sibling = {"lat": lat + 1 - 2 * core}

    def turned(which_lat, place):
        odd = lax.rem(which_lat, 2)
        return place + odd * (n_ten - 1 - 2 * place)

    part = turned(lat, ten)
    band = lat * n_ten + part

    def band_at(step):
        there = lax.rem(band + step + bands, bands)
        there_lat = there // n_ten
        return {"lat": there_lat, "tensor": turned(there_lat, lax.rem(there, n_ten))}

    def lon_at(step):
        return lax.rem(lon + step + n_lon, n_lon)

    def ten_at(step):
        return lax.rem(ten + step, n_ten)

    def far_first(i):
        return n_lon // 2 + ((i + 1) // 2) * (1 - 2 * lax.rem(i, 2))

    def by_core(i):
        return far_first(i + core * (n_lon - 2 - 2 * i))

    fetches = [
        pltpu.make_async_copy(source, target, fetch_sem.at[index])
        for index, (source, target) in enumerate(
            (
                (fields_hbm, fields),
                (w_qkv_hbm, w_qkv),
                (gain1_hbm, gain1),
                (dw_kernel_hbm, dw_kernel),
                (logit_scale_hbm, logit_scale),
                (attn_keep_hbm, attn_keep),
                (gain2_hbm, gain2),
                (mlp_keep_hbm, mlp_keep),
            )
        )
    ]
    for fetch in fetches[:3]:
        fetch.start()

    barrier = pltpu.get_barrier_semaphore()

    def greet(i, carry):
        pl.semaphore_signal(
            barrier, inc=1, device_id={"lon": lon_at(far_first(i))}, device_id_type=MESH
        )
        return carry

    lax.fori_loop(0, n_lon - 1, greet, 0)
    for step in range(1, n_ten):
        pl.semaphore_signal(
            barrier, inc=1, device_id={"tensor": ten_at(step)}, device_id_type=MESH
        )
    for step in (-1, 1):
        pl.semaphore_signal(barrier, inc=1, device_id=band_at(step), device_id_type=MESH)
    pl.semaphore_signal(barrier, inc=1, device_id=sibling, device_id_type=MESH)

    for fetch in fetches[3:]:
        fetch.start()

    proj_w[...] = jnp.zeros_like(proj_w)
    for fetch in fetches[:3]:
        fetch.wait()
    for head in range(heads):
        for which in range(3):
            proj_w[pl.ds(head * LANES + which * head_size, head_size), :] = w_qkv[which, head]
    normed = layer_norm(fields[...].reshape(rows * cols, channels).astype(f32), gain1[...])
    projected = lax.dot_general(
        normed, proj_w[...], (((1,), (1,)), ((), ())), preferred_element_type=f32
    ).astype(bf16)
    projected = projected.reshape(rows, groups, SUB, heads * LANES)
    for row in range(rows):
        for head in range(heads):
            place = spot_of[row]
            sent[place * heads + head] = projected[row, :, :, head * LANES : (head + 1) * LANES]

    pl.semaphore_wait(barrier, n_lon - 1 + n_ten - 1 + 3)

    def send_pair(i, carry):
        peer = lon_at(by_core(i))
        pltpu.make_async_remote_copy(
            src_ref=sent.at[peer],
            dst_ref=got.at[:, lon],
            send_sem=send_a,
            recv_sem=recv_a,
            device_id={"lon": peer},
            device_id_type=MESH,
        ).start()
        return carry

    lax.fori_loop(0, n_lon - 1, send_pair, 0)
    pltpu.make_async_copy(sent.at[lon], got.at[:, lon], recv_a).start()

    for step in range(1, n_ten):
        pl.semaphore_signal(
            go_sem, inc=1, device_id={"tensor": ten_at(step)}, device_id_type=MESH
        )
    for step in (-1, 1):
        pl.semaphore_signal(go_sem, inc=1, device_id=band_at(step), device_id_type=MESH)

    def half_of(ref):
        half = ref.shape[0] // 2
        return ref.at[pl.ds(core * half, half)]

    pairs_w = ((w_out, out_w), (w_up, up_w), (w_down, down_w))
    weight_copies, weight_passes, weight_own = [], [], []
    for kind, (mine, whole) in enumerate(pairs_w):
        for step in range(1, n_ten):
            copy = pltpu.make_async_remote_copy(
                src_ref=half_of(mine),
                dst_ref=half_of(whole.at[ten]),
                send_sem=send_w.at[kind, step - 1],
                recv_sem=recv_w.at[kind, step - 1],
                device_id={"tensor": ten_at(step)},
                device_id_type=MESH,
            )
            copy.start()
            weight_copies.append(copy)
            arrived = half_of(whole.at[ten_at(n_ten - step)])
            weight_passes.append(
                pltpu.make_async_remote_copy(
                    src_ref=arrived,
                    dst_ref=arrived,
                    send_sem=send_p.at[kind, step - 1],
                    recv_sem=recv_p.at[kind, step - 1],
                    device_id=sibling,
                    device_id_type=MESH,
                )
            )
        own = pltpu.make_async_copy(mine, whole.at[ten], own_w.at[kind])
        own.start()
        weight_own.append(own)

    def weights_here(kind):
        weight_own[kind].wait()
        for step in range(1, n_ten):
            weight_passes[kind * (n_ten - 1) + step - 1].wait_recv()

    own_part = pl.ds(part * quarter, quarter)
    side_copies = []
    for index, (step, start) in enumerate(((1, cols - SUB), (-1, 0))):
        copy = pltpu.make_async_remote_copy(
            src_ref=fields.at[own_part, pl.ds(start, SUB)],
            dst_ref=side.at[index],
            send_sem=send_s.at[index],
            recv_sem=recv_s.at[index],
            device_id={"lon": lon_at(step)},
            device_id_type=MESH,
        )
        copy.start()
        side_copies.append(copy)

    for fetch in fetches[3:]:
        fetch.wait()
    for row_off in range(size):
        line = dw_kernel[row_off].astype(f32)
        for col_off in range(size):
            for half in range(halves):
                taps[half, row_off * size + col_off] = jnp.broadcast_to(
                    line[col_off : col_off + 1, half * LANES : (half + 1) * LANES],
                    (SUB, LANES),
                )

    pltpu.make_async_copy(got, got, recv_a).wait()
    keys = groups * n_lon * SUB
    gathered = got[...].reshape(keys, LANES)
    wide = gathered.astype(f32)
    lane = lax.broadcasted_iota(jnp.int32, (keys, LANES), 1)
    at_keys = (lane >= head_size) & (lane < 2 * head_size)
    queries = jnp.where(at_keys, pltpu.roll(wide, head_size, 1), 0.0)
    by_group = queries.reshape(groups, n_lon, SUB, LANES)
    left_side = jnp.concatenate([by_group[-1, -1:], by_group[-1, :-1]], axis=0)
    right_side = jnp.concatenate([by_group[0, 1:], by_group[0, :1]], axis=0)
    place = lax.broadcasted_iota(jnp.int32, left_side.shape, 1)
    beside = jnp.where(place >= SUB // 2, left_side, right_side)
    span = n_lon * SUB
    queries = [by_group[group].reshape(span, LANES).astype(bf16) for group in range(groups)]
    queries.append(beside.reshape(span, LANES).astype(bf16))
    for group in range(groups + 1):
        low, high = group * head_size, (group + 1) * head_size
        shift = (low - 2 * head_size) % LANES
        moved = pltpu.roll(wide, shift, 1) if shift else wide
        inside = (lane >= low) & (lane < high)
        values[group, :, :LANES] = jnp.where(inside, moved, 0.0).astype(bf16)
        values[group, :, LANES:] = jnp.where(inside, 1.0, 0.0).astype(bf16)
    pair_head = lax.rem(lon, heads)
    pair_place = lon // heads
    scale = logit_scale[0]
    for head in range(1, heads):
        scale = jnp.where(pair_head == head, logit_scale[head], scale)
    coef = scale * (math.log2(math.e) / math.sqrt(head_size))
    pair_row = row_of[0]
    for index in range(1, rows):
        pair_row = jnp.where(pair_place == index, row_of[index], pair_row)
    owner = turned(lat, pair_row // quarter)
    slot_row = lax.rem(pair_row, quarter)
    slot_head = ten * heads + pair_head
    pl.semaphore_wait(go_sem, n_ten - 1 + 2)

    def send_back(peer, carry):
        @pl.when(peer != lon)
        def _():
            pltpu.make_async_remote_copy(
                src_ref=mixed.at[peer],
                dst_ref=joined.at[slot_row, slot_head],
                send_sem=send_b,
                recv_sem=recv_b,
                device_id={"lon": peer, "tensor": owner},
                device_id_type=MESH,
            ).start()

        return carry

    portion = n_lon // 2
    for start in range(0, n_lon, portion):
        total = jnp.zeros((portion * SUB, 2 * LANES), f32)
        for group in range(groups + 1):
            scores = lax.dot_general(
                queries[group][start * SUB : (start + portion) * SUB],
                gathered,
                (((1,), (1,)), ((), ())),
                preferred_element_type=f32,
            )
            top = jnp.max(scores, axis=-1, keepdims=True)
            weights = jnp.exp2((scores - top) * coef).astype(bf16)
            total = total + jnp.dot(weights, values[group], preferred_element_type=f32)
        mixed[pl.ds(start, portion)] = (
            (total[:, :LANES] / total[:, LANES:]).astype(bf16).reshape(portion, SUB, LANES)
        )
        lax.fori_loop(start, start + portion, send_back, 0)

    @pl.when(owner == ten)
    def _():
        pltpu.make_async_copy(mixed.at[lon], joined.at[slot_row, slot_head], recv_b).start()

    own_back = pltpu.make_async_remote_copy(
        src_ref=mixed.at[lon],
        dst_ref=joined.at[slot_row, slot_head],
        send_sem=send_b_own,
        recv_sem=recv_b,
        device_id={"tensor": owner},
        device_id_type=MESH,
    )

    @pl.when(owner != ten)
    def _():
        own_back.start()

    for copy, onward in zip(weight_copies, weight_passes):
        copy.wait_recv()
        onward.start()

    out_wide[...] = jnp.zeros_like(out_wide)
    weights_here(0)
    for head in range(all_heads):
        block = out_w[head // heads, head % heads]
        for group in range(groups + 1):
            out_wide[
                pl.ds(head * LANES + group * head_size, head_size),
                pl.ds(group * channels, channels),
            ] = block

    pltpu.make_async_copy(joined, joined, recv_b).wait()
    packed = jnp.concatenate(
        [joined[:, head].reshape(quarter * SUB, LANES) for head in range(all_heads)], axis=-1
    )
    attended = jnp.dot(packed, out_wide[...], preferred_element_type=f32)
    for copy in side_copies:
        copy.wait_recv()
    place = lax.broadcasted_iota(jnp.int32, (SUB, channels), 0)
    for row in range(quarter):
        at = part * quarter + row
        factor = attn_keep[pl.ds(at, 1), :].astype(f32) / keep_prob
        block = fields[at].astype(f32)
        for group in range(groups + 1):
            piece = attended[
                row * SUB : (row + 1) * SUB, group * channels : (group + 1) * channels
            ]
            if group < groups:
                base = block[group * SUB : (group + 1) * SUB]
            else:
                base = jnp.where(
                    place >= SUB // 2, side[0, row].astype(f32), side[1, row].astype(f32)
                )
            stream = (base + piece * factor).astype(bf16)
            if group < groups:
                ext[margin + row, pl.ds((group + 1) * SUB, SUB), :] = stream
            else:
                ext[margin + row, pl.ds(0, SUB), :] = stream

    middle = pl.ds(SUB, cols)
    halo_copies = []
    for index, (step, source, target) in enumerate(
        ((-1, margin, margin + quarter), (1, quarter, 0))
    ):
        copy = pltpu.make_async_remote_copy(
            src_ref=ext.at[pl.ds(source, margin)],
            dst_ref=ext.at[pl.ds(target, margin)],
            send_sem=send_h.at[index],
            recv_sem=recv_h.at[index],
            device_id=band_at(step),
            device_id_type=MESH,
        )
        halo_copies.append(copy)
    has_above, has_below = band > 0, band < bands - 1

    @pl.when(has_above)
    def _():
        halo_copies[0].start()

    @pl.when(has_below)
    def _():
        halo_copies[1].start()

    @pl.when(jnp.logical_not(has_above))
    def _():
        ext[pl.ds(0, margin)] = jnp.zeros((margin,) + ext.shape[1:], bf16)

    @pl.when(jnp.logical_not(has_below))
    def _():
        ext[pl.ds(margin + quarter, margin)] = jnp.zeros((margin,) + ext.shape[1:], bf16)

    @pl.when(has_above)
    def _():
        halo_copies[1].wait_recv()

    @pl.when(has_below)
    def _():
        halo_copies[0].wait_recv()

    for row in range(quarter + 2 * margin):
        line = ext[row].astype(f32)
        for half in range(halves):
            piece = line[:, half * LANES : (half + 1) * LANES]
            ext_f[half, row, pl.ds(0, cols + SUB), :] = piece
            ext_f[half, row, pl.ds(cols + SUB, SUB), :] = piece[:SUB]
    parts = []
    for half in range(halves):
        sums = [jnp.zeros((cols, LANES), f32) for _ in range(quarter)]
        for col_off in range(size):
            tap = [
                jnp.concatenate([taps[half, row_off * size + col_off]] * groups, axis=0)
                for row_off in range(size)
            ]
            for row in range(quarter + 2 * margin):
                line = ext_f[half, row, pl.ds(SUB - margin + col_off, cols), :]
                for i in range(quarter):
                    if 0 <= row - i < size:
                        sums[i] = sums[i] + tap[row - i] * line
        parts.append(jnp.concatenate(sums, axis=0))
    spatial = jnp.concatenate(parts, axis=-1).astype(bf16).astype(f32)

    normed2 = layer_norm(spatial, gain2[...])
    weights_here(1)
    weights_here(2)
    ffn = jnp.zeros((quarter * cols, channels), f32)
    for index in range(n_ten):
        inner = jnp.dot(normed2, up_w[index], preferred_element_type=f32)
        hidden = (0.5 * inner * (1.0 + lax.erf(inner * math.sqrt(0.5)))).astype(bf16)
        ffn = ffn + jnp.dot(hidden, down_w[index], preferred_element_type=f32)
    for row in range(quarter):
        factor = mlp_keep[pl.ds(part * quarter + row, 1), :].astype(f32) / keep_prob
        stream = ext[margin + row, middle, :].astype(f32)
        done[row] = (stream + ffn[row * cols : (row + 1) * cols] * factor).astype(bf16)

    out_copies = []
    for index in range(n_ten - 1):
        target = index + (index >= ten).astype(jnp.int32)
        slot = lax.rem(target - ten + n_ten - 1, n_ten)
        copy = pltpu.make_async_remote_copy(
            src_ref=done,
            dst_ref=out.at[own_part],
            send_sem=send_o.at[index],
            recv_sem=recv_o.at[slot],
            device_id={"tensor": target},
            device_id_type=MESH,
        )
        copy.start()
        out_copies.append(copy)
    own_out = pltpu.make_async_copy(done, out.at[own_part], send_o.at[n_ten - 1])
    own_out.start()

    @pl.when(has_above)
    def _():
        halo_copies[0].wait_send()

    @pl.when(has_below)
    def _():
        halo_copies[1].wait_send()

    pltpu.make_async_copy(sent.at[: n_lon - 1], sent.at[: n_lon - 1], send_a).wait()
    pltpu.make_async_copy(mixed.at[: n_lon - 1], mixed.at[: n_lon - 1], send_b).wait()

    @pl.when(owner != ten)
    def _():
        own_back.wait_send()

    for copy in weight_copies + weight_passes + side_copies + out_copies:
        copy.wait_send()
    own_out.wait()
    for slot in range(n_ten - 1):
        pltpu.make_async_copy(done, out.at[own_part], recv_o.at[slot]).wait()


def shards(sizes, fields, gain1, w_qkv, logit_scale, w_out, attn_keep, dw_kernel, gain2, w_up, w_down, mlp_keep):
    n_lat, n_lon, n_ten = sizes
    rows, cols, channels = fields.shape
    heads, head_size = w_qkv.shape[2:]
    hidden = w_up.shape[1]
    groups, quarter, size = cols // SUB, rows // n_ten, dw_kernel.shape[0]
    margin, halves = size // 2, channels // LANES
    span = quarter + 2 * margin
    hbm = pl.BlockSpec(memory_space=pltpu.HBM)
    dma = pltpu.SemaphoreType.DMA
    return pl.pallas_call(
        functools.partial(kernel, n_lat, n_lon, n_ten),
        out_shape=jax.ShapeDtypeStruct(fields.shape, bf16),
        in_specs=[hbm] * 11,
        out_specs=pl.BlockSpec(memory_space=pl.ANY),
        scratch_shapes=[
            pltpu.VMEM(fields.shape, bf16),
            pltpu.VMEM((1, channels), f32),
            pltpu.VMEM((3, heads, head_size, channels), bf16),
            pltpu.SMEM(logit_scale.shape, f32),
            pltpu.VMEM(attn_keep.shape, jnp.int32),
            pltpu.VMEM(dw_kernel.shape, bf16),
            pltpu.VMEM((1, channels), f32),
            pltpu.VMEM(mlp_keep.shape, jnp.int32),
            pltpu.VMEM((heads * LANES, channels), bf16),
            pltpu.VMEM((n_lon, groups, SUB, LANES), bf16),
            pltpu.VMEM((groups, n_lon, SUB, LANES), bf16),
            pltpu.VMEM((groups + 1, groups * n_lon * SUB, 2 * LANES), bf16),
            pltpu.VMEM((n_lon, SUB, LANES), bf16),
            pltpu.VMEM((quarter, heads * n_ten, SUB, LANES), bf16),
            pltpu.VMEM((n_ten,) + w_out.shape, bf16),
            pltpu.VMEM((heads * n_ten * LANES, (groups + 1) * channels), bf16),
            pltpu.VMEM((n_ten, channels, hidden), bf16),
            pltpu.VMEM((n_ten, hidden, channels), bf16),
            pltpu.VMEM((halves, size * size, SUB, LANES), f32),
            pltpu.VMEM((span, cols + SUB, channels), bf16),
            pltpu.VMEM((halves, span, cols + 2 * SUB, LANES), f32),
            pltpu.VMEM((2, quarter, SUB, channels), bf16),
            pltpu.VMEM((quarter, cols, channels), bf16),
            dma((8,)),
            pltpu.SemaphoreType.REGULAR,
            dma, dma, dma, dma, dma,
            dma((3, n_ten - 1)),
            dma((3, n_ten - 1)),
            dma((3, n_ten - 1)),
            dma((3, n_ten - 1)),
            dma((2,)),
            dma((2,)),
            dma((3,)),
            dma((2,)),
            dma((2,)),
            dma((n_ten,)),
            dma((n_ten - 1,)),
        ],
        compiler_params=pltpu.CompilerParams(
            collective_id=0, has_side_effects=True, vmem_limit_bytes=32 << 20
        ),
    )(
        *(
            pltpu.with_memory_space_constraint(operand, pltpu.HBM)
            for operand in (
                fields,
                gain1.reshape(1, channels),
                w_qkv.transpose(1, 2, 3, 0),
                logit_scale,
                w_out,
                attn_keep,
                dw_kernel,
                gain2.reshape(1, channels),
                w_up,
                w_down,
                mlp_keep,
            )
        )
    )


def solution(mesh):
    sizes = tuple(mesh.shape[axis] for axis in ("lat", "lon", "tensor"))
    placed = (
        P("lat", "lon", None),
        P(),
        P(None, None, "tensor", None),
        P("tensor"),
        P("tensor", None, None),
        P("lat", None),
        P(),
        P(),
        P(None, "tensor"),
        P("tensor", None),
        P("lat", None),
    )
    return jax.shard_map(
        functools.partial(shards, sizes),
        mesh=mesh,
        in_specs=placed,
        out_specs=P("lat", "lon", None),
        check_vma=False,
    )
```

```python
import functools
import math

import jax
import jax.numpy as jnp
from jax import lax
from jax.experimental import pallas as pl
from jax.experimental.pallas import tpu as pltpu
from jax.sharding import PartitionSpec as P

ln_eps = 1e-05
keep_prob = 0.9
LANES = 128
SUB = 8
MESH = pl.DeviceIdType.MESH
f32 = jnp.float32
bf16 = jnp.bfloat16


def layer_norm(values, gain):
    center = jnp.mean(values, axis=-1, keepdims=True)
    shifted = values - center
    spread = jnp.mean(jnp.square(shifted), axis=-1, keepdims=True)
    return (shifted * lax.rsqrt(spread + ln_eps) * gain).astype(bf16)


def kernel(
    n_lat,
    n_lon,
    n_ten,
    fields_hbm,
    gain1_hbm,
    w_qkv_hbm,
    logit_scale_hbm,
    w_out,
    attn_keep_hbm,
    dw_kernel_hbm,
    gain2_hbm,
    w_up,
    w_down,
    mlp_keep_hbm,
    out,
    fields,
    gain1,
    w_qkv,
    logit_scale,
    attn_keep,
    dw_kernel,
    gain2,
    mlp_keep,
    proj_w,
    sent,
    got,
    values,
    mixed,
    joined,
    out_w,
    up_w,
    down_w,
    taps,
    ext,
    ext_f,
    side,
    done,
    fetch_sem,
    go_sem,
    send_a,
    recv_a,
    send_b,
    send_b_own,
    recv_b,
    send_w,
    recv_w,
    send_p,
    recv_p,
    send_s,
    recv_s,
    own_w,
    send_h,
    recv_h,
    send_o,
    recv_o,
):
    rows, cols, channels = fields.shape
    heads = w_qkv.shape[1]
    head_size = w_qkv.shape[2]
    groups = cols // SUB
    quarter = rows // n_ten
    all_heads = heads * n_ten
    size = dw_kernel.shape[0]
    margin = size // 2
    halves = channels // LANES
    bands = n_lat * n_ten
    spot_of = (14, 1, 15, 0, 8, 7, 9, 6, 10, 5, 11, 4, 12, 3, 13, 2)
    row_of = (3, 1, 15, 13, 11, 9, 7, 5, 4, 6, 8, 10, 12, 14, 0, 2)

    lat = lax.axis_index("lat")
    lon = lax.axis_index("lon")
    ten = lax.axis_index("tensor")
    core = lax.rem(lat, 2)
    sibling = {"lat": lat + 1 - 2 * core}

    def turned(which_lat, place):
        odd = lax.rem(which_lat, 2)
        return place + odd * (n_ten - 1 - 2 * place)

    part = turned(lat, ten)
    band = lat * n_ten + part

    def band_at(step):
        there = lax.rem(band + step + bands, bands)
        there_lat = there // n_ten
        return {"lat": there_lat, "tensor": turned(there_lat, lax.rem(there, n_ten))}

    def lon_at(step):
        return lax.rem(lon + step + n_lon, n_lon)

    def ten_at(step):
        return lax.rem(ten + step, n_ten)

    def far_first(i):
        return n_lon // 2 + ((i + 1) // 2) * (1 - 2 * lax.rem(i, 2))

    def by_core(i):
        return far_first(i + core * (n_lon - 2 - 2 * i))

    fetches = [
        pltpu.make_async_copy(source, target, fetch_sem.at[index])
        for index, (source, target) in enumerate(
            (
                (fields_hbm, fields),
                (w_qkv_hbm, w_qkv),
                (gain1_hbm, gain1),
                (dw_kernel_hbm, dw_kernel),
                (logit_scale_hbm, logit_scale),
                (attn_keep_hbm, attn_keep),
                (gain2_hbm, gain2),
                (mlp_keep_hbm, mlp_keep),
            )
        )
    ]
    for fetch in fetches[:3]:
        fetch.start()

    barrier = pltpu.get_barrier_semaphore()

    def greet(i, carry):
        pl.semaphore_signal(
            barrier, inc=1, device_id={"lon": lon_at(far_first(i))}, device_id_type=MESH
        )
        return carry

    lax.fori_loop(0, n_lon - 1, greet, 0)
    for step in range(1, n_ten):
        pl.semaphore_signal(
            barrier, inc=1, device_id={"tensor": ten_at(step)}, device_id_type=MESH
        )
    for step in (-1, 1):
        pl.semaphore_signal(barrier, inc=1, device_id=band_at(step), device_id_type=MESH)
    pl.semaphore_signal(barrier, inc=1, device_id=sibling, device_id_type=MESH)

    for fetch in fetches[3:]:
        fetch.start()

    proj_w[...] = jnp.zeros_like(proj_w)
    for fetch in fetches[:3]:
        fetch.wait()
    for head in range(heads):
        for which in range(3):
            proj_w[pl.ds(head * LANES + which * head_size, head_size), :] = w_qkv[which, head]
    normed = layer_norm(fields[...].reshape(rows * cols, channels).astype(f32), gain1[...])
    projected = lax.dot_general(
        normed, proj_w[...], (((1,), (1,)), ((), ())), preferred_element_type=f32
    ).astype(bf16)
    projected = projected.reshape(rows, groups, SUB, heads * LANES)
    for row in range(rows):
        for head in range(heads):
            place = spot_of[row]
            sent[place * heads + head] = projected[row, :, :, head * LANES : (head + 1) * LANES]

    pl.semaphore_wait(barrier, n_lon - 1 + n_ten - 1 + 3)

    def send_pair(i, carry):
        peer = lon_at(by_core(i))
        pltpu.make_async_remote_copy(
            src_ref=sent.at[peer],
            dst_ref=got.at[:, lon],
            send_sem=send_a,
            recv_sem=recv_a,
            device_id={"lon": peer},
            device_id_type=MESH,
        ).start()
        return carry

    lax.fori_loop(0, n_lon - 1, send_pair, 0)
    pltpu.make_async_copy(sent.at[lon], got.at[:, lon], recv_a).start()

    for step in range(1, n_ten):
        pl.semaphore_signal(
            go_sem, inc=1, device_id={"tensor": ten_at(step)}, device_id_type=MESH
        )
    for step in (-1, 1):
        pl.semaphore_signal(go_sem, inc=1, device_id=band_at(step), device_id_type=MESH)

    def half_of(ref):
        half = ref.shape[0] // 2
        return ref.at[pl.ds(core * half, half)]

    pairs_w = ((w_out, out_w), (w_up, up_w), (w_down, down_w))
    weight_copies, weight_passes, weight_own = [], [], []
    for kind, (mine, whole) in enumerate(pairs_w):
        for step in range(1, n_ten):
            copy = pltpu.make_async_remote_copy(
                src_ref=half_of(mine),
                dst_ref=half_of(whole.at[ten]),
                send_sem=send_w.at[kind, step - 1],
                recv_sem=recv_w.at[kind, step - 1],
                device_id={"tensor": ten_at(step)},
                device_id_type=MESH,
            )
            copy.start()
            weight_copies.append(copy)
            arrived = half_of(whole.at[ten_at(n_ten - step)])
            weight_passes.append(
                pltpu.make_async_remote_copy(
                    src_ref=arrived,
                    dst_ref=arrived,
                    send_sem=send_p.at[kind, step - 1],
                    recv_sem=recv_p.at[kind, step - 1],
                    device_id=sibling,
                    device_id_type=MESH,
                )
            )
        own = pltpu.make_async_copy(mine, whole.at[ten], own_w.at[kind])
        own.start()
        weight_own.append(own)

    def weights_here(kind):
        weight_own[kind].wait()
        for step in range(1, n_ten):
            weight_passes[kind * (n_ten - 1) + step - 1].wait_recv()

    own_part = pl.ds(part * quarter, quarter)
    side_copies = []
    for index, (step, start) in enumerate(((1, cols - SUB), (-1, 0))):
        copy = pltpu.make_async_remote_copy(
            src_ref=fields.at[own_part, pl.ds(start, SUB)],
            dst_ref=side.at[index],
            send_sem=send_s.at[index],
            recv_sem=recv_s.at[index],
            device_id={"lon": lon_at(step)},
            device_id_type=MESH,
        )
        copy.start()
        side_copies.append(copy)

    for fetch in fetches[3:]:
        fetch.wait()
    for row_off in range(size):
        line = dw_kernel[row_off].astype(f32)
        for col_off in range(size):
            for half in range(halves):
                taps[half, row_off * size + col_off] = jnp.broadcast_to(
                    line[col_off : col_off + 1, half * LANES : (half + 1) * LANES],
                    (SUB, LANES),
                )

    pltpu.make_async_copy(got, got, recv_a).wait()
    keys = groups * n_lon * SUB
    gathered = got[...].reshape(keys, LANES)
    wide = gathered.astype(f32)
    lane = lax.broadcasted_iota(jnp.int32, (keys, LANES), 1)
    at_keys = (lane >= head_size) & (lane < 2 * head_size)
    queries = jnp.where(at_keys, pltpu.roll(wide, head_size, 1), 0.0)
    by_group = queries.reshape(groups, n_lon, SUB, LANES)
    left_side = jnp.concatenate([by_group[-1, -1:], by_group[-1, :-1]], axis=0)
    right_side = jnp.concatenate([by_group[0, 1:], by_group[0, :1]], axis=0)
    place = lax.broadcasted_iota(jnp.int32, left_side.shape, 1)
    beside = jnp.where(place >= SUB // 2, left_side, right_side)
    span = n_lon * SUB
    queries = [by_group[group].reshape(span, LANES).astype(bf16) for group in range(groups)]
    queries.append(beside.reshape(span, LANES).astype(bf16))
    for group in range(groups + 1):
        low, high = group * head_size, (group + 1) * head_size
        shift = (low - 2 * head_size) % LANES
        moved = pltpu.roll(wide, shift, 1) if shift else wide
        inside = (lane >= low) & (lane < high)
        values[group, :, :LANES] = jnp.where(inside, moved, 0.0).astype(bf16)
        values[group, :, LANES:] = jnp.where(inside, 1.0, 0.0).astype(bf16)
    pair_head = lax.rem(lon, heads)
    pair_place = lon // heads
    scale = logit_scale[0]
    for head in range(1, heads):
        scale = jnp.where(pair_head == head, logit_scale[head], scale)
    coef = scale * (math.log2(math.e) / math.sqrt(head_size))
    pair_row = row_of[0]
    for index in range(1, rows):
        pair_row = jnp.where(pair_place == index, row_of[index], pair_row)
    owner = turned(lat, pair_row // quarter)
    slot_row = lax.rem(pair_row, quarter)
    slot_head = ten * heads + pair_head
    pl.semaphore_wait(go_sem, n_ten - 1 + 2)

    def send_back(peer, carry):
        @pl.when(peer != lon)
        def _():
            pltpu.make_async_remote_copy(
                src_ref=mixed.at[peer],
                dst_ref=joined.at[slot_row, slot_head],
                send_sem=send_b,
                recv_sem=recv_b,
                device_id={"lon": peer, "tensor": owner},
                device_id_type=MESH,
            ).start()

        return carry

    portion = n_lon // 2
    for start in range(0, n_lon, portion):
        total = jnp.zeros((portion * SUB, 2 * LANES), f32)
        for group in range(groups + 1):
            scores = lax.dot_general(
                queries[group][start * SUB : (start + portion) * SUB],
                gathered,
                (((1,), (1,)), ((), ())),
                preferred_element_type=f32,
            )
            top = jnp.max(scores, axis=-1, keepdims=True)
            weights = jnp.exp2((scores - top) * coef).astype(bf16)
            total = total + jnp.dot(weights, values[group], preferred_element_type=f32)
        mixed[pl.ds(start, portion)] = (
            (total[:, :LANES] / total[:, LANES:]).astype(bf16).reshape(portion, SUB, LANES)
        )
        lax.fori_loop(start, start + portion, send_back, 0)

    @pl.when(owner == ten)
    def _():
        pltpu.make_async_copy(mixed.at[lon], joined.at[slot_row, slot_head], recv_b).start()

    own_back = pltpu.make_async_remote_copy(
        src_ref=mixed.at[lon],
        dst_ref=joined.at[slot_row, slot_head],
        send_sem=send_b_own,
        recv_sem=recv_b,
        device_id={"tensor": owner},
        device_id_type=MESH,
    )

    @pl.when(owner != ten)
    def _():
        own_back.start()

    for copy, onward in zip(weight_copies, weight_passes):
        copy.wait_recv()
        onward.start()

    weights_here(0)
    out_all = out_w[...].reshape(all_heads * head_size, channels)
    lane = lax.broadcasted_iota(jnp.int32, (quarter * SUB, LANES), 1)
    per_tile = LANES // head_size
    pltpu.make_async_copy(joined, joined, recv_b).wait()
    tiles = [
        joined[:, head].reshape(quarter * SUB, LANES).astype(f32) for head in range(all_heads)
    ]
    lines = []
    for group in range(groups + 1):
        line = []
        for start in range(0, all_heads, per_tile):
            merged = None
            for k in range(per_tile):
                shift = (k - group) * head_size % LANES
                moved = tiles[start + k]
                moved = pltpu.roll(moved, shift, 1) if shift else moved
                merged = jnp.where(lane >= k * head_size, moved, merged) if k else moved
            line.append(merged)
        lines.append(jnp.concatenate(line, axis=-1))
    attended = jnp.dot(
        jnp.concatenate(lines, axis=0).astype(bf16), out_all, preferred_element_type=f32
    )
    for copy in side_copies:
        copy.wait_recv()
    place = lax.broadcasted_iota(jnp.int32, (SUB, channels), 0)
    for row in range(quarter):
        at = part * quarter + row
        factor = attn_keep[pl.ds(at, 1), :].astype(f32) / keep_prob
        block = fields[at].astype(f32)
        for group in range(groups + 1):
            at_piece = (group * quarter + row) * SUB
            piece = attended[at_piece : at_piece + SUB]
            if group < groups:
                base = block[group * SUB : (group + 1) * SUB]
            else:
                base = jnp.where(
                    place >= SUB // 2, side[0, row].astype(f32), side[1, row].astype(f32)
                )
            stream = (base + piece * factor).astype(bf16)
            if group < groups:
                ext[margin + row, pl.ds((group + 1) * SUB, SUB), :] = stream
            else:
                ext[margin + row, pl.ds(0, SUB), :] = stream

    middle = pl.ds(SUB, cols)
    halo_copies = []
    for index, (step, source, target) in enumerate(
        ((-1, margin, margin + quarter), (1, quarter, 0))
    ):
        copy = pltpu.make_async_remote_copy(
            src_ref=ext.at[pl.ds(source, margin)],
            dst_ref=ext.at[pl.ds(target, margin)],
            send_sem=send_h.at[index],
            recv_sem=recv_h.at[index],
            device_id=band_at(step),
            device_id_type=MESH,
        )
        halo_copies.append(copy)
    has_above, has_below = band > 0, band < bands - 1

    @pl.when(has_above)
    def _():
        halo_copies[0].start()

    @pl.when(has_below)
    def _():
        halo_copies[1].start()

    @pl.when(jnp.logical_not(has_above))
    def _():
        ext[pl.ds(0, margin)] = jnp.zeros((margin,) + ext.shape[1:], bf16)

    @pl.when(jnp.logical_not(has_below))
    def _():
        ext[pl.ds(margin + quarter, margin)] = jnp.zeros((margin,) + ext.shape[1:], bf16)

    @pl.when(has_above)
    def _():
        halo_copies[1].wait_recv()

    @pl.when(has_below)
    def _():
        halo_copies[0].wait_recv()

    for row in range(quarter + 2 * margin):
        line = ext[row].astype(f32)
        for half in range(halves):
            piece = line[:, half * LANES : (half + 1) * LANES]
            ext_f[half, row, pl.ds(0, cols + SUB), :] = piece
            ext_f[half, row, pl.ds(cols + SUB, SUB), :] = piece[:SUB]
    parts = []
    for half in range(halves):
        sums = [jnp.zeros((cols, LANES), f32) for _ in range(quarter)]
        for col_off in range(size):
            tap = [
                jnp.concatenate([taps[half, row_off * size + col_off]] * groups, axis=0)
                for row_off in range(size)
            ]
            for row in range(quarter + 2 * margin):
                line = ext_f[half, row, pl.ds(SUB - margin + col_off, cols), :]
                for i in range(quarter):
                    if 0 <= row - i < size:
                        sums[i] = sums[i] + tap[row - i] * line
        parts.append(jnp.concatenate(sums, axis=0))
    spatial = jnp.concatenate(parts, axis=-1).astype(bf16).astype(f32)

    normed2 = layer_norm(spatial, gain2[...])
    weights_here(1)
    weights_here(2)
    ffn = jnp.zeros((quarter * cols, channels), f32)
    for index in range(n_ten):
        inner = jnp.dot(normed2, up_w[index], preferred_element_type=f32)
        hidden = (0.5 * inner * (1.0 + lax.erf(inner * math.sqrt(0.5)))).astype(bf16)
        ffn = ffn + jnp.dot(hidden, down_w[index], preferred_element_type=f32)
    for row in range(quarter):
        factor = mlp_keep[pl.ds(part * quarter + row, 1), :].astype(f32) / keep_prob
        stream = ext[margin + row, middle, :].astype(f32)
        done[row] = (stream + ffn[row * cols : (row + 1) * cols] * factor).astype(bf16)

    out_copies = []
    for index in range(n_ten - 1):
        target = index + (index >= ten).astype(jnp.int32)
        slot = lax.rem(target - ten + n_ten - 1, n_ten)
        copy = pltpu.make_async_remote_copy(
            src_ref=done,
            dst_ref=out.at[own_part],
            send_sem=send_o.at[index],
            recv_sem=recv_o.at[slot],
            device_id={"tensor": target},
            device_id_type=MESH,
        )
        copy.start()
        out_copies.append(copy)
    own_out = pltpu.make_async_copy(done, out.at[own_part], send_o.at[n_ten - 1])
    own_out.start()

    @pl.when(has_above)
    def _():
        halo_copies[0].wait_send()

    @pl.when(has_below)
    def _():
        halo_copies[1].wait_send()

    pltpu.make_async_copy(sent.at[: n_lon - 1], sent.at[: n_lon - 1], send_a).wait()
    pltpu.make_async_copy(mixed.at[: n_lon - 1], mixed.at[: n_lon - 1], send_b).wait()

    @pl.when(owner != ten)
    def _():
        own_back.wait_send()

    for copy in weight_copies + weight_passes + side_copies + out_copies:
        copy.wait_send()
    own_out.wait()
    for slot in range(n_ten - 1):
        pltpu.make_async_copy(done, out.at[own_part], recv_o.at[slot]).wait()


def shards(sizes, fields, gain1, w_qkv, logit_scale, w_out, attn_keep, dw_kernel, gain2, w_up, w_down, mlp_keep):
    n_lat, n_lon, n_ten = sizes
    rows, cols, channels = fields.shape
    heads, head_size = w_qkv.shape[2:]
    hidden = w_up.shape[1]
    groups, quarter, size = cols // SUB, rows // n_ten, dw_kernel.shape[0]
    margin, halves = size // 2, channels // LANES
    span = quarter + 2 * margin
    hbm = pl.BlockSpec(memory_space=pltpu.HBM)
    dma = pltpu.SemaphoreType.DMA
    return pl.pallas_call(
        functools.partial(kernel, n_lat, n_lon, n_ten),
        out_shape=jax.ShapeDtypeStruct(fields.shape, bf16),
        in_specs=[hbm] * 11,
        out_specs=pl.BlockSpec(memory_space=pl.ANY),
        scratch_shapes=[
            pltpu.VMEM(fields.shape, bf16),
            pltpu.VMEM((1, channels), f32),
            pltpu.VMEM((3, heads, head_size, channels), bf16),
            pltpu.SMEM(logit_scale.shape, f32),
            pltpu.VMEM(attn_keep.shape, jnp.int32),
            pltpu.VMEM(dw_kernel.shape, bf16),
            pltpu.VMEM((1, channels), f32),
            pltpu.VMEM(mlp_keep.shape, jnp.int32),
            pltpu.VMEM((heads * LANES, channels), bf16),
            pltpu.VMEM((n_lon, groups, SUB, LANES), bf16),
            pltpu.VMEM((groups, n_lon, SUB, LANES), bf16),
            pltpu.VMEM((groups + 1, groups * n_lon * SUB, 2 * LANES), bf16),
            pltpu.VMEM((n_lon, SUB, LANES), bf16),
            pltpu.VMEM((quarter, heads * n_ten, SUB, LANES), bf16),
            pltpu.VMEM((n_ten,) + w_out.shape, bf16),
            pltpu.VMEM((n_ten, channels, hidden), bf16),
            pltpu.VMEM((n_ten, hidden, channels), bf16),
            pltpu.VMEM((halves, size * size, SUB, LANES), f32),
            pltpu.VMEM((span, cols + SUB, channels), bf16),
            pltpu.VMEM((halves, span, cols + 2 * SUB, LANES), f32),
            pltpu.VMEM((2, quarter, SUB, channels), bf16),
            pltpu.VMEM((quarter, cols, channels), bf16),
            dma((8,)),
            pltpu.SemaphoreType.REGULAR,
            dma, dma, dma, dma, dma,
            dma((3, n_ten - 1)),
            dma((3, n_ten - 1)),
            dma((3, n_ten - 1)),
            dma((3, n_ten - 1)),
            dma((2,)),
            dma((2,)),
            dma((3,)),
            dma((2,)),
            dma((2,)),
            dma((n_ten,)),
            dma((n_ten - 1,)),
        ],
        compiler_params=pltpu.CompilerParams(
            collective_id=0, has_side_effects=True, vmem_limit_bytes=32 << 20
        ),
    )(
        *(
            pltpu.with_memory_space_constraint(operand, pltpu.HBM)
            for operand in (
                fields,
                gain1.reshape(1, channels),
                w_qkv.transpose(1, 2, 3, 0),
                logit_scale,
                w_out,
                attn_keep,
                dw_kernel,
                gain2.reshape(1, channels),
                w_up,
                w_down,
                mlp_keep,
            )
        )
    )


def solution(mesh):
    sizes = tuple(mesh.shape[axis] for axis in ("lat", "lon", "tensor"))
    placed = (
        P("lat", "lon", None),
        P(),
        P(None, None, "tensor", None),
        P("tensor"),
        P("tensor", None, None),
        P("lat", None),
        P(),
        P(),
        P(None, "tensor"),
        P("tensor", None),
        P("lat", None),
    )
    return jax.shard_map(
        functools.partial(shards, sizes),
        mesh=mesh,
        in_specs=placed,
        out_specs=P("lat", "lon", None),
        check_vma=False,
    )
```

```python
import functools
import math

import jax
import jax.numpy as jnp
from jax import lax
from jax.experimental import pallas as pl
from jax.experimental.pallas import tpu as pltpu
from jax.sharding import PartitionSpec as P

ln_eps = 1e-05
keep_prob = 0.9
LANES = 128
SUB = 8
MESH = pl.DeviceIdType.MESH
f32 = jnp.float32
bf16 = jnp.bfloat16


def layer_norm(values, gain):
    center = jnp.mean(values, axis=-1, keepdims=True)
    shifted = values - center
    spread = jnp.mean(jnp.square(shifted), axis=-1, keepdims=True)
    return (shifted * lax.rsqrt(spread + ln_eps) * gain).astype(bf16)


def kernel(
    n_lat,
    n_lon,
    n_ten,
    fields_hbm,
    gain1_hbm,
    w_qkv_hbm,
    logit_scale_hbm,
    w_out,
    attn_keep_hbm,
    dw_kernel_hbm,
    gain2_hbm,
    w_up,
    w_down,
    mlp_keep_hbm,
    out,
    fields,
    gain1,
    w_qkv,
    logit_scale,
    attn_keep,
    dw_kernel,
    gain2,
    mlp_keep,
    proj_w,
    sent,
    got,
    values,
    mixed,
    joined,
    out_w,
    up_w,
    down_w,
    taps,
    ext,
    ext_f,
    side,
    done,
    fetch_sem,
    go_sem,
    send_a,
    recv_a,
    send_b,
    send_b_own,
    recv_b,
    send_w,
    recv_w,
    send_p,
    recv_p,
    send_s,
    recv_s,
    own_w,
    send_h,
    recv_h,
    send_o,
    recv_o,
):
    rows, cols, channels = fields.shape
    heads = w_qkv.shape[1]
    head_size = w_qkv.shape[2]
    groups = cols // SUB
    quarter = rows // n_ten
    all_heads = heads * n_ten
    size = dw_kernel.shape[0]
    margin = size // 2
    halves = channels // LANES
    bands = n_lat * n_ten
    spot_of = (14, 1, 15, 0, 8, 7, 9, 6, 10, 5, 11, 4, 12, 3, 13, 2)
    row_of = (3, 1, 15, 13, 11, 9, 7, 5, 4, 6, 8, 10, 12, 14, 0, 2)

    lat = lax.axis_index("lat")
    lon = lax.axis_index("lon")
    ten = lax.axis_index("tensor")
    core = lax.rem(lat, 2)
    sibling = {"lat": lat + 1 - 2 * core}

    def turned(which_lat, place):
        odd = lax.rem(which_lat, 2)
        return place + odd * (n_ten - 1 - 2 * place)

    part = turned(lat, ten)
    band = lat * n_ten + part

    def band_at(step):
        there = lax.rem(band + step + bands, bands)
        there_lat = there // n_ten
        return {"lat": there_lat, "tensor": turned(there_lat, lax.rem(there, n_ten))}

    def lon_at(step):
        return lax.rem(lon + step + n_lon, n_lon)

    def ten_at(step):
        return lax.rem(ten + step, n_ten)

    def far_first(i):
        return n_lon // 2 + ((i + 1) // 2) * (1 - 2 * lax.rem(i, 2))

    def by_core(i):
        return far_first(i + core * (n_lon - 2 - 2 * i))

    fetches = [
        pltpu.make_async_copy(source, target, fetch_sem.at[index])
        for index, (source, target) in enumerate(
            (
                (fields_hbm, fields),
                (w_qkv_hbm, w_qkv),
                (gain1_hbm, gain1),
                (dw_kernel_hbm, dw_kernel),
                (logit_scale_hbm, logit_scale),
                (attn_keep_hbm, attn_keep),
                (gain2_hbm, gain2),
                (mlp_keep_hbm, mlp_keep),
            )
        )
    ]
    for fetch in fetches[:3]:
        fetch.start()

    barrier = pltpu.get_barrier_semaphore()

    def greet(i, carry):
        pl.semaphore_signal(
            barrier, inc=1, device_id={"lon": lon_at(far_first(i))}, device_id_type=MESH
        )
        return carry

    lax.fori_loop(0, n_lon - 1, greet, 0)
    for step in range(1, n_ten):
        pl.semaphore_signal(
            barrier, inc=1, device_id={"tensor": ten_at(step)}, device_id_type=MESH
        )
    for step in (-1, 1):
        pl.semaphore_signal(barrier, inc=1, device_id=band_at(step), device_id_type=MESH)
    pl.semaphore_signal(barrier, inc=1, device_id=sibling, device_id_type=MESH)

    for fetch in fetches[3:]:
        fetch.start()

    proj_w[...] = jnp.zeros_like(proj_w)
    for fetch in fetches[:3]:
        fetch.wait()
    for head in range(heads):
        for which in range(3):
            proj_w[pl.ds(head * LANES + which * head_size, head_size), :] = w_qkv[which, head]
    normed = layer_norm(fields[...].reshape(rows * cols, channels).astype(f32), gain1[...])
    projected = lax.dot_general(
        normed, proj_w[...], (((1,), (1,)), ((), ())), preferred_element_type=f32
    ).astype(bf16)
    projected = projected.reshape(rows, groups, SUB, heads * LANES)
    for row in range(rows):
        for head in range(heads):
            place = spot_of[row]
            sent[place * heads + head] = projected[row, :, :, head * LANES : (head + 1) * LANES]

    pl.semaphore_wait(barrier, n_lon - 1 + n_ten - 1 + 3)

    def send_pair(i, carry):
        peer = lon_at(by_core(i))
        pltpu.make_async_remote_copy(
            src_ref=sent.at[peer],
            dst_ref=got.at[:, lon],
            send_sem=send_a,
            recv_sem=recv_a,
            device_id={"lon": peer},
            device_id_type=MESH,
        ).start()
        return carry

    lax.fori_loop(0, n_lon - 1, send_pair, 0)
    pltpu.make_async_copy(sent.at[lon], got.at[:, lon], recv_a).start()

    for step in range(1, n_ten):
        pl.semaphore_signal(
            go_sem, inc=1, device_id={"tensor": ten_at(step)}, device_id_type=MESH
        )
    for step in (-1, 1):
        pl.semaphore_signal(go_sem, inc=1, device_id=band_at(step), device_id_type=MESH)

    def half_of(ref):
        half = ref.shape[0] // 2
        return ref.at[pl.ds(core * half, half)]

    pairs_w = ((w_out, out_w), (w_up, up_w), (w_down, down_w))
    weight_copies, weight_passes, weight_own = [], [], []
    for kind, (mine, whole) in enumerate(pairs_w):
        for step in range(1, n_ten):
            copy = pltpu.make_async_remote_copy(
                src_ref=half_of(mine),
                dst_ref=half_of(whole.at[ten]),
                send_sem=send_w.at[kind, step - 1],
                recv_sem=recv_w.at[kind, step - 1],
                device_id={"tensor": ten_at(step)},
                device_id_type=MESH,
            )
            copy.start()
            weight_copies.append(copy)
            arrived = half_of(whole.at[ten_at(n_ten - step)])
            weight_passes.append(
                pltpu.make_async_remote_copy(
                    src_ref=arrived,
                    dst_ref=arrived,
                    send_sem=send_p.at[kind, step - 1],
                    recv_sem=recv_p.at[kind, step - 1],
                    device_id=sibling,
                    device_id_type=MESH,
                )
            )
        own = pltpu.make_async_copy(mine, whole.at[ten], own_w.at[kind])
        own.start()
        weight_own.append(own)

    def weights_here(kind):
        weight_own[kind].wait()
        for step in range(1, n_ten):
            weight_passes[kind * (n_ten - 1) + step - 1].wait_recv()

    own_part = pl.ds(part * quarter, quarter)
    side_copies = []
    for index, (step, start) in enumerate(((1, cols - SUB), (-1, 0))):
        copy = pltpu.make_async_remote_copy(
            src_ref=fields.at[own_part, pl.ds(start, SUB)],
            dst_ref=side.at[index],
            send_sem=send_s.at[index],
            recv_sem=recv_s.at[index],
            device_id={"lon": lon_at(step)},
            device_id_type=MESH,
        )
        copy.start()
        side_copies.append(copy)

    for fetch in fetches[3:]:
        fetch.wait()
    for row_off in range(size):
        line = dw_kernel[row_off].astype(f32)
        for col_off in range(size):
            for half in range(halves):
                taps[half, row_off * size + col_off] = jnp.broadcast_to(
                    line[col_off : col_off + 1, half * LANES : (half + 1) * LANES],
                    (SUB, LANES),
                )

    pltpu.make_async_copy(got, got, recv_a).wait()
    keys = groups * n_lon * SUB
    gathered = got[...].reshape(keys, LANES)
    wide = gathered.astype(f32)
    lane = lax.broadcasted_iota(jnp.int32, (keys, LANES), 1)
    at_keys = (lane >= head_size) & (lane < 2 * head_size)
    queries = jnp.where(at_keys, pltpu.roll(wide, head_size, 1), 0.0)
    by_group = queries.reshape(groups, n_lon, SUB, LANES)
    left_side = jnp.concatenate([by_group[-1, -1:], by_group[-1, :-1]], axis=0)
    right_side = jnp.concatenate([by_group[0, 1:], by_group[0, :1]], axis=0)
    place = lax.broadcasted_iota(jnp.int32, left_side.shape, 1)
    beside = jnp.where(place >= SUB // 2, left_side, right_side)
    span = n_lon * SUB
    queries = [by_group[group].reshape(span, LANES).astype(bf16) for group in range(groups)]
    queries.append(beside.reshape(span, LANES).astype(bf16))
    for group in range(groups + 1):
        low, high = group * head_size, (group + 1) * head_size
        shift = (low - 2 * head_size) % LANES
        moved = pltpu.roll(wide, shift, 1) if shift else wide
        inside = (lane >= low) & (lane < high)
        values[group, :, :LANES] = jnp.where(inside, moved, 0.0).astype(bf16)
        values[group, :, LANES:] = jnp.where(inside, 1.0, 0.0).astype(bf16)
    pair_head = lax.rem(lon, heads)
    pair_place = lon // heads
    scale = logit_scale[0]
    for head in range(1, heads):
        scale = jnp.where(pair_head == head, logit_scale[head], scale)
    coef = scale * (math.log2(math.e) / math.sqrt(head_size))
    pair_row = row_of[0]
    for index in range(1, rows):
        pair_row = jnp.where(pair_place == index, row_of[index], pair_row)
    owner = turned(lat, pair_row // quarter)
    slot_row = lax.rem(pair_row, quarter)
    slot_head = ten * heads + pair_head
    pl.semaphore_wait(go_sem, n_ten - 1 + 2)

    def send_back(peer, carry):
        @pl.when(peer != lon)
        def _():
            pltpu.make_async_remote_copy(
                src_ref=mixed.at[peer],
                dst_ref=joined.at[slot_row, slot_head],
                send_sem=send_b,
                recv_sem=recv_b,
                device_id={"lon": peer, "tensor": owner},
                device_id_type=MESH,
            ).start()

        return carry

    portion = n_lon // 4
    for start in range(0, n_lon, portion):
        total = jnp.zeros((portion * SUB, 2 * LANES), f32)
        for group in range(groups + 1):
            scores = lax.dot_general(
                queries[group][start * SUB : (start + portion) * SUB],
                gathered,
                (((1,), (1,)), ((), ())),
                preferred_element_type=f32,
            )
            top = jnp.max(scores, axis=-1, keepdims=True)
            weights = jnp.exp2((scores - top) * coef).astype(bf16)
            total = total + jnp.dot(weights, values[group], preferred_element_type=f32)
        mixed[pl.ds(start, portion)] = (
            (total[:, :LANES] / total[:, LANES:]).astype(bf16).reshape(portion, SUB, LANES)
        )
        lax.fori_loop(start, start + portion, send_back, 0)

    @pl.when(owner == ten)
    def _():
        pltpu.make_async_copy(mixed.at[lon], joined.at[slot_row, slot_head], recv_b).start()

    own_back = pltpu.make_async_remote_copy(
        src_ref=mixed.at[lon],
        dst_ref=joined.at[slot_row, slot_head],
        send_sem=send_b_own,
        recv_sem=recv_b,
        device_id={"tensor": owner},
        device_id_type=MESH,
    )

    @pl.when(owner != ten)
    def _():
        own_back.start()

    for copy, onward in zip(weight_copies, weight_passes):
        copy.wait_recv()
        onward.start()

    weights_here(0)
    out_all = out_w[...].reshape(all_heads * head_size, channels)
    lane = lax.broadcasted_iota(jnp.int32, (quarter * SUB, LANES), 1)
    per_tile = LANES // head_size
    pltpu.make_async_copy(joined, joined, recv_b).wait()
    tiles = [
        joined[:, head].reshape(quarter * SUB, LANES).astype(f32) for head in range(all_heads)
    ]
    lines = []
    for group in range(groups + 1):
        line = []
        for start in range(0, all_heads, per_tile):
            merged = None
            for k in range(per_tile):
                shift = (k - group) * head_size % LANES
                moved = tiles[start + k]
                moved = pltpu.roll(moved, shift, 1) if shift else moved
                merged = jnp.where(lane >= k * head_size, moved, merged) if k else moved
            line.append(merged)
        lines.append(jnp.concatenate(line, axis=-1))
    attended = jnp.dot(
        jnp.concatenate(lines, axis=0).astype(bf16), out_all, preferred_element_type=f32
    )
    for copy in side_copies:
        copy.wait_recv()
    place = lax.broadcasted_iota(jnp.int32, (SUB, channels), 0)
    for row in range(quarter):
        at = part * quarter + row
        factor = attn_keep[pl.ds(at, 1), :].astype(f32) / keep_prob
        block = fields[at].astype(f32)
        for group in range(groups + 1):
            at_piece = (group * quarter + row) * SUB
            piece = attended[at_piece : at_piece + SUB]
            if group < groups:
                base = block[group * SUB : (group + 1) * SUB]
            else:
                base = jnp.where(
                    place >= SUB // 2, side[0, row].astype(f32), side[1, row].astype(f32)
                )
            stream = (base + piece * factor).astype(bf16)
            if group < groups:
                ext[margin + row, pl.ds((group + 1) * SUB, SUB), :] = stream
            else:
                ext[margin + row, pl.ds(0, SUB), :] = stream

    middle = pl.ds(SUB, cols)
    halo_copies = []
    for index, (step, source, target) in enumerate(
        ((-1, margin, margin + quarter), (1, quarter, 0))
    ):
        copy = pltpu.make_async_remote_copy(
            src_ref=ext.at[pl.ds(source, margin)],
            dst_ref=ext.at[pl.ds(target, margin)],
            send_sem=send_h.at[index],
            recv_sem=recv_h.at[index],
            device_id=band_at(step),
            device_id_type=MESH,
        )
        halo_copies.append(copy)
    has_above, has_below = band > 0, band < bands - 1

    @pl.when(has_above)
    def _():
        halo_copies[0].start()

    @pl.when(has_below)
    def _():
        halo_copies[1].start()

    @pl.when(jnp.logical_not(has_above))
    def _():
        ext[pl.ds(0, margin)] = jnp.zeros((margin,) + ext.shape[1:], bf16)

    @pl.when(jnp.logical_not(has_below))
    def _():
        ext[pl.ds(margin + quarter, margin)] = jnp.zeros((margin,) + ext.shape[1:], bf16)

    @pl.when(has_above)
    def _():
        halo_copies[1].wait_recv()

    @pl.when(has_below)
    def _():
        halo_copies[0].wait_recv()

    for row in range(quarter + 2 * margin):
        line = ext[row].astype(f32)
        for half in range(halves):
            piece = line[:, half * LANES : (half + 1) * LANES]
            ext_f[half, row, pl.ds(0, cols + SUB), :] = piece
            ext_f[half, row, pl.ds(cols + SUB, SUB), :] = piece[:SUB]
    parts = []
    for half in range(halves):
        sums = [jnp.zeros((cols, LANES), f32) for _ in range(quarter)]
        for col_off in range(size):
            tap = [
                jnp.concatenate([taps[half, row_off * size + col_off]] * groups, axis=0)
                for row_off in range(size)
            ]
            for row in range(quarter + 2 * margin):
                line = ext_f[half, row, pl.ds(SUB - margin + col_off, cols), :]
                for i in range(quarter):
                    if 0 <= row - i < size:
                        sums[i] = sums[i] + tap[row - i] * line
        parts.append(jnp.concatenate(sums, axis=0))
    spatial = jnp.concatenate(parts, axis=-1).astype(bf16).astype(f32)

    normed2 = layer_norm(spatial, gain2[...])
    weights_here(1)
    weights_here(2)
    ffn = jnp.zeros((quarter * cols, channels), f32)
    for index in range(n_ten):
        inner = jnp.dot(normed2, up_w[index], preferred_element_type=f32)
        hidden = (0.5 * inner * (1.0 + lax.erf(inner * math.sqrt(0.5)))).astype(bf16)
        ffn = ffn + jnp.dot(hidden, down_w[index], preferred_element_type=f32)
    for row in range(quarter):
        factor = mlp_keep[pl.ds(part * quarter + row, 1), :].astype(f32) / keep_prob
        stream = ext[margin + row, middle, :].astype(f32)
        done[row] = (stream + ffn[row * cols : (row + 1) * cols] * factor).astype(bf16)

    out_copies = []
    for index in range(n_ten - 1):
        target = index + (index >= ten).astype(jnp.int32)
        slot = lax.rem(target - ten + n_ten - 1, n_ten)
        copy = pltpu.make_async_remote_copy(
            src_ref=done,
            dst_ref=out.at[own_part],
            send_sem=send_o.at[index],
            recv_sem=recv_o.at[slot],
            device_id={"tensor": target},
            device_id_type=MESH,
        )
        copy.start()
        out_copies.append(copy)
    own_out = pltpu.make_async_copy(done, out.at[own_part], send_o.at[n_ten - 1])
    own_out.start()

    @pl.when(has_above)
    def _():
        halo_copies[0].wait_send()

    @pl.when(has_below)
    def _():
        halo_copies[1].wait_send()

    pltpu.make_async_copy(sent.at[: n_lon - 1], sent.at[: n_lon - 1], send_a).wait()
    pltpu.make_async_copy(mixed.at[: n_lon - 1], mixed.at[: n_lon - 1], send_b).wait()

    @pl.when(owner != ten)
    def _():
        own_back.wait_send()

    for copy in weight_copies + weight_passes + side_copies + out_copies:
        copy.wait_send()
    own_out.wait()
    for slot in range(n_ten - 1):
        pltpu.make_async_copy(done, out.at[own_part], recv_o.at[slot]).wait()


def shards(sizes, fields, gain1, w_qkv, logit_scale, w_out, attn_keep, dw_kernel, gain2, w_up, w_down, mlp_keep):
    n_lat, n_lon, n_ten = sizes
    rows, cols, channels = fields.shape
    heads, head_size = w_qkv.shape[2:]
    hidden = w_up.shape[1]
    groups, quarter, size = cols // SUB, rows // n_ten, dw_kernel.shape[0]
    margin, halves = size // 2, channels // LANES
    span = quarter + 2 * margin
    hbm = pl.BlockSpec(memory_space=pltpu.HBM)
    dma = pltpu.SemaphoreType.DMA
    return pl.pallas_call(
        functools.partial(kernel, n_lat, n_lon, n_ten),
        out_shape=jax.ShapeDtypeStruct(fields.shape, bf16),
        in_specs=[hbm] * 11,
        out_specs=pl.BlockSpec(memory_space=pl.ANY),
        scratch_shapes=[
            pltpu.VMEM(fields.shape, bf16),
            pltpu.VMEM((1, channels), f32),
            pltpu.VMEM((3, heads, head_size, channels), bf16),
            pltpu.SMEM(logit_scale.shape, f32),
            pltpu.VMEM(attn_keep.shape, jnp.int32),
            pltpu.VMEM(dw_kernel.shape, bf16),
            pltpu.VMEM((1, channels), f32),
            pltpu.VMEM(mlp_keep.shape, jnp.int32),
            pltpu.VMEM((heads * LANES, channels), bf16),
            pltpu.VMEM((n_lon, groups, SUB, LANES), bf16),
            pltpu.VMEM((groups, n_lon, SUB, LANES), bf16),
            pltpu.VMEM((groups + 1, groups * n_lon * SUB, 2 * LANES), bf16),
            pltpu.VMEM((n_lon, SUB, LANES), bf16),
            pltpu.VMEM((quarter, heads * n_ten, SUB, LANES), bf16),
            pltpu.VMEM((n_ten,) + w_out.shape, bf16),
            pltpu.VMEM((n_ten, channels, hidden), bf16),
            pltpu.VMEM((n_ten, hidden, channels), bf16),
            pltpu.VMEM((halves, size * size, SUB, LANES), f32),
            pltpu.VMEM((span, cols + SUB, channels), bf16),
            pltpu.VMEM((halves, span, cols + 2 * SUB, LANES), f32),
            pltpu.VMEM((2, quarter, SUB, channels), bf16),
            pltpu.VMEM((quarter, cols, channels), bf16),
            dma((8,)),
            pltpu.SemaphoreType.REGULAR,
            dma, dma, dma, dma, dma,
            dma((3, n_ten - 1)),
            dma((3, n_ten - 1)),
            dma((3, n_ten - 1)),
            dma((3, n_ten - 1)),
            dma((2,)),
            dma((2,)),
            dma((3,)),
            dma((2,)),
            dma((2,)),
            dma((n_ten,)),
            dma((n_ten - 1,)),
        ],
        compiler_params=pltpu.CompilerParams(
            collective_id=0, has_side_effects=True, vmem_limit_bytes=32 << 20
        ),
    )(
        *(
            pltpu.with_memory_space_constraint(operand, pltpu.HBM)
            for operand in (
                fields,
                gain1.reshape(1, channels),
                w_qkv.transpose(1, 2, 3, 0),
                logit_scale,
                w_out,
                attn_keep,
                dw_kernel,
                gain2.reshape(1, channels),
                w_up,
                w_down,
                mlp_keep,
            )
        )
    )


def solution(mesh):
    sizes = tuple(mesh.shape[axis] for axis in ("lat", "lon", "tensor"))
    placed = (
        P("lat", "lon", None),
        P(),
        P(None, None, "tensor", None),
        P("tensor"),
        P("tensor", None, None),
        P("lat", None),
        P(),
        P(),
        P(None, "tensor"),
        P("tensor", None),
        P("lat", None),
    )
    return jax.shard_map(
        functools.partial(shards, sizes),
        mesh=mesh,
        in_specs=placed,
        out_specs=P("lat", "lon", None),
        check_vma=False,
    )
```
